256 devices in a mesh: bond: 64 (over z, x, core), row: 4 (over y).
Axes of the slice: x: 4, y: 4, z: 8, core: 2. Of those that a mesh axis runs over, the one named last changes fastest.
Arguments:
- left_site: bfloat16 [131072, 1024], P(('bond', 'row')), may hold values from -6 to 6
- right_site: bfloat16 [65536, 2048], P(('bond', 'row')), may hold values from -0.1875 to 0.1875
- gate: float32 [4, 4], replicated, may hold values from -3 to 3
- omega: bfloat16 [2048, 1024], P(('bond', 'row')), may hold values from -0.125 to 0.125
Outputs:
- left_new: bfloat16 [131072, 1024], P(('bond', 'row'))
- right_new: bfloat16 [65536, 2048], P(('bond', 'row'))
- odd_pair: bfloat16 [131072, 2048], P(('bond', 'row'))
The draws below stay inside these ranges and needn't reach their ends.
All inputs are finite; a program needn't handle non-finite values.
Results may differ from the reference program's by a relative error of at most 0.03.
Values may be sent and summed in bfloat16 or wider, within the bound.
No kernel may reach another device: no remote copies, remote signals or barrier semaphores. Data moves between devices by JAX's collectives and lax.ppermute only.
A program may use at most 128 MiB of HBM per device.

```python
import math
import jax
import jax.numpy as jnp
from jax import lax

C = 1024
K = 1024
BONDS = 64


def block_levels(rng, dims, shards, least, largest):
    factor_of = 1.0
    for position, parts in shards:
        heights = jax.random.uniform(jax.random.fold_in(jax.random.fold_in(rng, 6), position), (parts,), jnp.float32, least / len(shards), largest / len(shards))
        factor_of = factor_of * jnp.repeat(jnp.exp(heights), dims[position] // parts).reshape((-1,) + (1,) * (len(dims) - 1 - position))
    return factor_of


def noise(rng, shape, scale, bound, shards=(), kind=jnp.bfloat16):
    values = jax.random.normal(rng, shape, jnp.float32) * scale
    if len(shards) > 0:
        values = block_levels(rng, shape, shards, -0.22, 0.18) * values
    return jnp.clip(values, min=-bound, max=bound).astype(kind)


def setup_inputs(seed: int = 0) -> dict:
    key_list = jax.random.split(jax.random.key(seed), 5)
    return {
        "left_site": noise(key_list[0], (BONDS * 2 * C, C), 1.0, 6.0, ((0, 256),)),
        "right_site": noise(key_list[1], (BONDS * C, 2 * C), C ** -0.5, 0.1875, ((0, 256),)),
        "gate": noise(key_list[2], (4, 4), 0.5, 3.0, (), jnp.float32),
        "omega": noise(key_list[3], (2 * C, K), (2 * C) ** -0.5, 0.125, ((0, 256),)),
    }


def one_bond(pair_in, gate, omega):
    left_one, right_one = pair_in
    product = jnp.dot(left_one.astype(jnp.float32), right_one.astype(jnp.float32), preferred_element_type=jnp.float32)
    mixed = jnp.einsum('stuv,auvc->astc', gate.reshape(2, 2, 2, 2).astype(jnp.float32), product.reshape(C, 2, 2, 2 * C // 2))
    theta = mixed.reshape(2 * C, 2 * C).astype(jnp.bfloat16)
    sketch = jnp.dot(theta.astype(jnp.float32), omega.astype(jnp.float32), preferred_element_type=jnp.float32)
    gram = jnp.dot(sketch.T, sketch, precision=lax.Precision.HIGHEST) / (2.0 * C)
    diag_mean = jnp.trace(gram) / K
    lower = jnp.linalg.cholesky(gram + 0.01 * diag_mean * jnp.eye(K, dtype=gram.dtype))
    basis = lax.linalg.triangular_solve(lower, sketch, left_side=False, lower=True, transpose_a=True)
    left_out = basis.astype(jnp.bfloat16)
    right_out = (jnp.dot(left_out.T.astype(jnp.float32), theta.astype(jnp.float32), preferred_element_type=jnp.float32) * (1.0 / math.sqrt(2.0 * C))).astype(jnp.bfloat16)
    return (left_out, right_out)

def odd_bond(pair_in):
    right_one, left_next = pair_in
    rows_view = right_one.reshape(2 * K, C)
    cols_view = left_next.reshape(C, 2 * K)
    result = jnp.dot(rows_view.astype(jnp.float32), cols_view.astype(jnp.float32), preferred_element_type=jnp.float32) * (1.0 / math.sqrt(1.0 * C))
    return result.astype(jnp.bfloat16)

def reference(left_site, right_site, gate, omega):
    lefts = left_site.reshape(BONDS, 2 * C, C)
    rights = right_site.reshape(BONDS, C, 2 * C)
    left_out, right_out = lax.map(lambda pair_in: one_bond(pair_in, gate, omega), (lefts, rights))
    shifted = jnp.concatenate([left_out[1:], jnp.zeros((1, 2 * C, K), jnp.bfloat16)], axis=0)
    odd_pair = lax.map(odd_bond, (right_out, shifted))
    return (left_out.reshape(BONDS * 2 * C, K), right_out.reshape(BONDS * K, 2 * C), odd_pair.reshape(BONDS * 2 * K, 2 * K))
```

```python
import functools
import math

import jax
import jax.numpy as jnp
from jax import lax
from jax.experimental import pallas as pl
from jax.experimental.pallas import tpu as pltpu
from jax.sharding import Mesh
from jax.sharding import PartitionSpec as P

BOND_ROW = ("bond_0", "bond_1", "bond_2", "row")
BOND = ("bond_0", "bond_1", "bond_2")
NB = 128
VMEM_LIMIT = 56 * 1024 * 1024


def sub_row(x, c):
    return jnp.broadcast_to(x[c:c+1, :], x.shape)
def lane_col(x, c):
    return jnp.broadcast_to(x[:, c:c+1], x.shape)
def diag_inverse(block):
    groups = NB // 8
    sub = lax.broadcasted_iota(jnp.int32, (8, NB), 0)
    lane = lax.broadcasted_iota(jnp.int32, (8, NB), 1)
    rows = [block[8*r:8*r+8, :] for r in range(groups)]
    er = [jnp.where(lane == sub + 8*r, 1.0, 0.0).astype(jnp.float32) for r in range(groups)]
    out = []
    for p in range(groups):
        cols = [lane_col(rows[p], 8*p+c) for c in range(8)]
        ahead = {r: [lane_col(rows[r], 8*p+c) for c in range(8)] for r in range(p+1, groups)}
        R, E = rows[p], er[p]
        raw = E; pv = cols[0]
        for c in range(8):
            here = sub == c
            rc = 1.0 / sub_row(cols[c], c)
            m = jnp.where(here, -rc, cols[c]*rc)
            if c:
                raw = jnp.where(here, E, raw); pv = jnp.where(here, cols[c], pv)
            if p + 1 < groups:
                R = jnp.where(here, 0.0, R) - m*sub_row(R, c)
            E = jnp.where(here, 0.0, E) - m*sub_row(E, c)
            for k in range(c+1, 8):
                cols[k] = jnp.where(here, 0.0, cols[k]) - m*sub_row(cols[k], c)
        out.append(raw * lax.rsqrt(pv))
        if p + 1 < groups:
            rb = [sub_row(R, c) for c in range(8)]; eb = [sub_row(E, c) for c in range(8)]
            for r in range(p+1, groups):
                a, e = rows[r], er[r]
                for c in range(8):
                    a = a - ahead[r][c]*rb[c]
                    e = e - ahead[r][c]*eb[c]
                rows[r], er[r] = a, e
    return jnp.concatenate(out, axis=0)
def hi_lo(x):
    hi = x.astype(jnp.bfloat16)
    return hi, (x - hi.astype(jnp.float32)).astype(jnp.bfloat16)
NT = (((1,), (1,)), ((), ()))
NN = (((1,), (0,)), ((), ()))
def mm3(ah, al, bh, bl, dims):
    d = functools.partial(lax.dot_general, dimension_numbers=dims, preferred_element_type=jnp.float32)
    return d(ah, bh) + (d(ah, bl) + d(al, bh))
def chol_kernel(rows_summed, g_ref, yh_ref, yl_ref, lh, ll, d_ref, inv_ref, cpre, epre):
    n = g_ref.shape[0]
    nblk = n // NB
    i0 = lax.broadcasted_iota(jnp.int32, (NB, NB), 0)
    i1 = lax.broadcasted_iota(jnp.int32, (NB, NB), 1)
    eye = jnp.where(i0 == i1, 1.0, 0.0).astype(jnp.float32)
    tot = jnp.zeros((NB, NB), jnp.float32)
    for b in range(nblk):
        tot = tot + g_ref[b*NB:(b+1)*NB, b*NB:(b+1)*NB]*eye
    trace = jnp.sum(tot)
    tv = jnp.full((8, NB), trace)
    alpha = (n / tv)[0:1, :]
    scale = lax.rsqrt(tv * (1.0/(rows_summed*n)))[0:1, :]
    lh[...] = jnp.zeros_like(lh); ll[...] = jnp.zeros_like(ll)
    yh_ref[...] = jnp.zeros_like(yh_ref); yl_ref[...] = jnp.zeros_like(yl_ref)
    d_ref[...] = g_ref[0:NB, 0:NB]*alpha + 0.01*eye
    cpre[...] = jnp.zeros_like(cpre)
    epre[...] = jnp.zeros_like(epre)
    inv_ref[...] = jnp.zeros_like(inv_ref)
    rowid = lax.broadcasted_iota(jnp.int32, (n, NB), 0)
    def finish(b):
        prev = pl.multiple_of(b*NB, NB)
        ih, il = hi_lo(inv_ref[...])
        epre[:, pl.ds(prev, NB)] = eye*scale
        eh, el = hi_lo(epre[...])
        yh, yl = hi_lo(mm3(ih, il, eh, el, NN))
        yh_ref[pl.ds(prev, NB), :] = yh
        yl_ref[pl.ds(prev, NB), :] = yl
        return ih, il, prev
    def body(b, carry):
        block = d_ref[...]
        inv = diag_inverse(block)
        prevb = jnp.maximum(b-1, 0)
        ih, il, prev = finish(prevb)
        ch, cl = hi_lo(cpre[...])
        panel = jnp.where(rowid >= b*NB, mm3(ch, cl, ih, il, NT), 0.0)
        ph, plo = hi_lo(panel)
        lh[:, pl.ds(prev, NB)] = ph
        ll[:, pl.ds(prev, NB)] = plo
        cur = pl.multiple_of(b*NB, NB)
        rh, rl = lh[pl.ds(cur, NB), :], ll[pl.ds(cur, NB), :]
        col = g_ref[:, pl.ds(cur, NB)]*alpha - mm3(lh[...], ll[...], rh, rl, NT)
        cpre[...] = col
        epre[...] = -mm3(rh, rl, yh_ref[...], yl_ref[...], NN)
        nxt = pl.multiple_of(jnp.minimum(b+1, nblk-1)*NB, NB)
        nh, nl = lh[pl.ds(nxt, NB), :], ll[pl.ds(nxt, NB), :]
        dpre = g_ref[pl.ds(nxt, NB), pl.ds(nxt, NB)]*alpha + 0.01*eye - mm3(nh, nl, nh, nl, NT)
        inv_ref[...] = inv
        vh, vl = hi_lo(inv)
        xh, xl = hi_lo(cpre[pl.ds(nxt, NB), :])
        th, tl = hi_lo(mm3(xh, xl, vh, vl, NT))
        d_ref[...] = dpre - mm3(th, tl, th, tl, NT)
        return carry
    lax.fori_loop(0, nblk, body, 0)
    finish(nblk-1)
def chol_inverse(gram_sum, rows_summed):
    n = gram_sum.shape[0]
    return pl.pallas_call(
        functools.partial(chol_kernel, rows_summed),
        out_shape=[jax.ShapeDtypeStruct((n, n), jnp.bfloat16)]*2,
        in_specs=[pl.BlockSpec(memory_space=pltpu.VMEM)],
        out_specs=[pl.BlockSpec(memory_space=pltpu.VMEM)]*2,
        scratch_shapes=[pltpu.VMEM((n,n),jnp.bfloat16)]*2+[pltpu.VMEM((NB,NB),jnp.float32)]*2+[pltpu.VMEM((n,NB),jnp.float32),pltpu.VMEM((NB,n),jnp.float32)],
        name="chol_inverse",
        compiler_params=pltpu.CompilerParams(vmem_limit_bytes=VMEM_LIMIT),
    )(gram_sum)


def in_vmem():
    return pl.BlockSpec(memory_space=pltpu.VMEM)


def chunk_kernel(gate_ref, a_ref, b_ref, om_ref, gin_ref, th_ref, s_ref, g_ref):
    half = om_ref.shape[0] // 2
    width = 512
    for c0 in range(0, half, width):
        p = {}
        for u in range(2):
            for v in range(2):
                p[u, v] = jnp.dot(
                    a_ref[u],
                    b_ref[:, v * half + c0 : v * half + c0 + width],
                    preferred_element_type=jnp.float32,
                )
        for s in range(2):
            for t in range(2):
                mixed = None
                for u in range(2):
                    for v in range(2):
                        term = gate_ref[2 * s + t, 2 * u + v] * p[u, v]
                        mixed = term if mixed is None else mixed + term
                th_ref[s, :, t * half + c0 : t * half + c0 + width] = mixed.astype(jnp.bfloat16)
    total = gin_ref[...]
    for s in range(2):
        sk = jnp.dot(th_ref[s], om_ref[...], preferred_element_type=jnp.float32).astype(jnp.bfloat16)
        s_ref[s] = sk
        total = total + lax.dot_general(
            sk, sk, (((0,), (0,)), ((), ())), preferred_element_type=jnp.float32
        )
    g_ref[...] = total


def theta_chunk(gate, a, b_full, om, gram):
    rows = a.shape[1]
    width = b_full.shape[1]
    kept = om.shape[1]
    return pl.pallas_call(
        chunk_kernel,
        out_shape=[
            jax.ShapeDtypeStruct((2, rows, width), jnp.bfloat16),
            jax.ShapeDtypeStruct((2, rows, kept), jnp.bfloat16),
            jax.ShapeDtypeStruct((kept, kept), jnp.float32),
        ],
        in_specs=[pl.BlockSpec(memory_space=pltpu.SMEM)] + [in_vmem()] * 4,
        out_specs=[in_vmem()] * 3,
        input_output_aliases={4: 2},
        name="theta_chunk",
        cost_estimate=pl.CostEstimate(flops=10 * 10**9, transcendentals=0, bytes_accessed=12 * 2**20),
        compiler_params=pltpu.CompilerParams(vmem_limit_bytes=VMEM_LIMIT),
    )(gate, a, b_full, om, gram)


def rot(block, axis, distance):
    count = lax.axis_size(axis)
    return lax.ppermute(block, axis, [(i, (i + distance) % count) for i in range(count)])


def from_behind(block):
    count = lax.axis_size(BOND)
    return lax.ppermute(block, BOND, [(i + 1, i) for i in range(count - 1)])


def place(whole, block, index, dim):
    starts = [0] * whole.ndim
    starts[dim] = index
    return lax.dynamic_update_slice(whole, block, tuple(starts))


def gather_omega(omega, row, x, core):
    rows, kept = omega.shape
    n_row, n_x, n_z = lax.axis_size("row"), lax.axis_size("bond_1"), lax.axis_size("bond_0")
    by_row = jnp.zeros((n_row, rows, kept), omega.dtype)
    by_row = place(by_row, omega[None], row, 0)
    for d in range(1, n_row):
        by_row = place(by_row, rot(omega, "row", d)[None], (row - d) % n_row, 0)
    strip = by_row.reshape(n_row * rows, kept)
    by_z = lax.all_gather(strip, "bond_0", axis=0)
    left, right = rot(by_z, "bond_1", 1), rot(by_z, "bond_1", -1)
    far = jnp.concatenate(
        [rot(left[: n_z // 2], "bond_1", 1), rot(right[n_z // 2 :], "bond_1", -1)], axis=0
    )
    mine = jnp.zeros((n_z, n_x) + strip.shape, omega.dtype)
    for block, d in ((by_z, 0), (left, 1), (right, -1), (far, 2)):
        mine = place(mine, block[:, None], (x - d) % n_x, 1)
    other = rot(mine, "bond_2", 1)
    whole = jnp.stack([jnp.where(core == 0, mine, other), jnp.where(core == 0, other, mine)], axis=2)
    return whole.reshape(-1, kept)


def shards(left_site, right_site, gate, omega):
    row_count, bond_width = left_site.shape
    own = right_site.shape[0]
    kept_rank = omega.shape[1]
    n_row = lax.axis_size("row")
    row = lax.axis_index("row")
    a0 = left_site.reshape(own, 2, bond_width).transpose(1, 0, 2)
    bl, br = rot(right_site, "row", 1), rot(right_site, "row", -1)
    om = gather_omega(omega, row, lax.axis_index("bond_1"), lax.axis_index("bond_2"))
    al, ar = rot(a0, "row", 1), rot(a0, "row", -1)
    bo1 = rot(bl[: own // 2], "row", 1)
    bo2 = rot(br[own // 2 :], "row", -1)
    ao = jnp.stack([rot(al[0], "row", 1), rot(ar[1], "row", -1)])
    b_full = jnp.zeros((n_row * own, right_site.shape[1]), right_site.dtype)
    b_full = place(b_full, right_site, row * own, 0)
    b_full = place(b_full, bl, (row - 1) % n_row * own, 0)
    b_full = place(b_full, br, (row + 1) % n_row * own, 0)
    b_full = place(b_full, bo1, (row + 2) % n_row * own, 0)
    b_full = place(b_full, bo2, (row + 2) % n_row * own + own // 2, 0)

    gram = jnp.zeros((kept_rank, kept_rank), jnp.float32)
    thetas, sketches = [], []
    for a in (a0, al, ar, ao):
        th, sk, gram = theta_chunk(gate, a, b_full, om, gram)
        thetas.append(th)
        sketches.append(sk)
    next_sketch = [from_behind(sk) for sk in sketches]
    yh, yl = chol_inverse(gram, 2.0 * bond_width)
    next_inv = from_behind(yh)

    f32 = functools.partial(lax.dot_general, preferred_element_type=jnp.float32)
    nt = (((1,), (1,)), ((), ()))
    own_h = lax.dynamic_slice(yh, (row * own, 0), (own, kept_rank))
    own_l = lax.dynamic_slice(yl, (row * own, 0), (own, kept_rank))
    right_sum = 0.0
    for sk, th in zip(sketches, thetas):
        flat = sk.reshape(2 * own, kept_rank)
        basis = (f32(flat, own_h, nt) + f32(flat, own_l, nt)).astype(jnp.bfloat16)
        right_sum = right_sum + f32(basis, th.reshape(2 * own, -1), (((0,), (0,)), ((), ())))
    right_new = (right_sum * (1.0 / math.sqrt(2.0 * bond_width))).astype(jnp.bfloat16)

    flat = sketches[0].reshape(2 * own, kept_rank)
    left_new = (f32(flat, yh, nt) + f32(flat, yl, nt)).astype(jnp.bfloat16)
    left_new = left_new.reshape(2, own, kept_rank).transpose(1, 0, 2).reshape(row_count, kept_rank)

    view = right_new.reshape(2 * own, bond_width)
    mid = [0.0, 0.0]
    for sk, d in zip(next_sketch, (0, -1, 1, 2)):
        part = lax.dynamic_slice(view, (0, (row + d) % n_row * own), (2 * own, own))
        for s in range(2):
            mid[s] = mid[s] + f32(part, sk[s], (((1,), (0,)), ((), ())))
    odd = []
    for s in range(2):
        mh, ml = hi_lo(mid[s])
        odd.append((f32(mh, next_inv, nt) + f32(ml, next_inv, nt)) * (1.0 / math.sqrt(1.0 * bond_width)))
    odd_pair = jnp.concatenate(odd, axis=1).astype(jnp.bfloat16)
    return (left_new, right_new, odd_pair)


def solution(mesh):
    torus = Mesh(
        mesh.devices.reshape(8, 4, 2, mesh.shape["row"]), ("bond_0", "bond_1", "bond_2", "row")
    )
    in_specs = (P(BOND_ROW, None), P(BOND_ROW, None), P(), P(BOND_ROW, None))
    out_specs = (P(BOND_ROW, None), P(BOND_ROW, None), P(BOND_ROW, None))
    return jax.shard_map(
        shards, mesh=torus, in_specs=in_specs, out_specs=out_specs, check_vma=False
    )
```

```python
import functools
import math

import jax
import jax.numpy as jnp
from jax import lax
from jax.experimental import pallas as pl
from jax.experimental.pallas import tpu as pltpu
from jax.sharding import Mesh
from jax.sharding import PartitionSpec as P

BOND_ROW = ("bond_0", "bond_1", "bond_2", "row")
BOND = ("bond_0", "bond_1", "bond_2")
NB = 128


def sub_row(x, c):
    return jnp.broadcast_to(x[c:c+1, :], x.shape)
def lane_col(x, c):
    return jnp.broadcast_to(x[:, c:c+1], x.shape)
def diag_inverse(block):
    groups = NB // 8
    sub = lax.broadcasted_iota(jnp.int32, (8, NB), 0)
    lane = lax.broadcasted_iota(jnp.int32, (8, NB), 1)
    rows = [block[8*r:8*r+8, :] for r in range(groups)]
    er = [jnp.where(lane == sub + 8*r, 1.0, 0.0).astype(jnp.float32) for r in range(groups)]
    out = []
    for p in range(groups):
        cols = [lane_col(rows[p], 8*p+c) for c in range(8)]
        ahead = {r: [lane_col(rows[r], 8*p+c) for c in range(8)] for r in range(p+1, groups)}
        R, E = rows[p], er[p]
        raw = E; pv = cols[0]
        for c in range(8):
            here = sub == c
            rc = 1.0 / sub_row(cols[c], c)
            m = jnp.where(here, -rc, cols[c]*rc)
            if c:
                raw = jnp.where(here, E, raw); pv = jnp.where(here, cols[c], pv)
            if p + 1 < groups:
                R = jnp.where(here, 0.0, R) - m*sub_row(R, c)
            E = jnp.where(here, 0.0, E) - m*sub_row(E, c)
            for k in range(c+1, 8):
                cols[k] = jnp.where(here, 0.0, cols[k]) - m*sub_row(cols[k], c)
        out.append(raw * lax.rsqrt(pv))
        if p + 1 < groups:
            rb = [sub_row(R, c) for c in range(8)]; eb = [sub_row(E, c) for c in range(8)]
            for r in range(p+1, groups):
                a, e = rows[r], er[r]
                for c in range(8):
                    a = a - ahead[r][c]*rb[c]
                    e = e - ahead[r][c]*eb[c]
                rows[r], er[r] = a, e
    return jnp.concatenate(out, axis=0)
def hi_lo(x):
    hi = x.astype(jnp.bfloat16)
    return hi, (x - hi.astype(jnp.float32)).astype(jnp.bfloat16)
NT = (((1,), (1,)), ((), ()))
NN = (((1,), (0,)), ((), ()))
def mm3(ah, al, bh, bl, dims):
    d = functools.partial(lax.dot_general, dimension_numbers=dims, preferred_element_type=jnp.float32)
    return d(ah, bh) + (d(ah, bl) + d(al, bh))
def chol_kernel(rows_summed, g_ref, yh_ref, yl_ref, packed_ref, lh, ll, d_ref, inv_ref, cpre, epre):
    n = g_ref.shape[0]
    nblk = n // NB
    i0 = lax.broadcasted_iota(jnp.int32, (NB, NB), 0)
    i1 = lax.broadcasted_iota(jnp.int32, (NB, NB), 1)
    eye = jnp.where(i0 == i1, 1.0, 0.0).astype(jnp.float32)
    tot = jnp.zeros((NB, NB), jnp.float32)
    for b in range(nblk):
        tot = tot + g_ref[b*NB:(b+1)*NB, b*NB:(b+1)*NB]*eye
    trace = jnp.sum(tot)
    tv = jnp.full((8, NB), trace)
    alpha = (n / tv)[0:1, :]
    scale = lax.rsqrt(tv * (1.0/(rows_summed*n)))[0:1, :]
    lh[...] = jnp.zeros_like(lh); ll[...] = jnp.zeros_like(ll)
    yh_ref[...] = jnp.zeros_like(yh_ref); yl_ref[...] = jnp.zeros_like(yl_ref)
    d_ref[...] = g_ref[0:NB, 0:NB]*alpha + 0.01*eye
    cpre[...] = jnp.zeros_like(cpre)
    epre[...] = jnp.zeros_like(epre)
    inv_ref[...] = jnp.zeros_like(inv_ref)
    rowid = lax.broadcasted_iota(jnp.int32, (n, NB), 0)
    def finish(b):
        prev = pl.multiple_of(b*NB, NB)
        ih, il = hi_lo(inv_ref[...])
        epre[:, pl.ds(prev, NB)] = eye*scale
        eh, el = hi_lo(epre[...])
        yh, yl = hi_lo(mm3(ih, il, eh, el, NN))
        yh_ref[pl.ds(prev, NB), :] = yh
        yl_ref[pl.ds(prev, NB), :] = yl
        return ih, il, prev
    def body(b, carry):
        block = d_ref[...]
        inv = diag_inverse(block)
        prevb = jnp.maximum(b-1, 0)
        ih, il, prev = finish(prevb)
        ch, cl = hi_lo(cpre[...])
        panel = jnp.where(rowid >= b*NB, mm3(ch, cl, ih, il, NT), 0.0)
        ph, plo = hi_lo(panel)
        lh[:, pl.ds(prev, NB)] = ph
        ll[:, pl.ds(prev, NB)] = plo
        cur = pl.multiple_of(b*NB, NB)
        rh, rl = lh[pl.ds(cur, NB), :], ll[pl.ds(cur, NB), :]
        col = g_ref[:, pl.ds(cur, NB)]*alpha - mm3(lh[...], ll[...], rh, rl, NT)
        cpre[...] = col
        epre[...] = -mm3(rh, rl, yh_ref[...], yl_ref[...], NN)
        nxt = pl.multiple_of(jnp.minimum(b+1, nblk-1)*NB, NB)
        nh, nl = lh[pl.ds(nxt, NB), :], ll[pl.ds(nxt, NB), :]
        dpre = g_ref[pl.ds(nxt, NB), pl.ds(nxt, NB)]*alpha + 0.01*eye - mm3(nh, nl, nh, nl, NT)
        inv_ref[...] = inv
        vh, vl = hi_lo(inv)
        xh, xl = hi_lo(cpre[pl.ds(nxt, NB), :])
        th, tl = hi_lo(mm3(xh, xl, vh, vl, NT))
        d_ref[...] = dpre - mm3(th, tl, th, tl, NT)
        return carry
    lax.fori_loop(0, nblk, body, 0)
    finish(nblk-1)
    q = n // 4
    packed_ref[:q, :n] = yh_ref[3*q:, :]
    packed_ref[:q, n:] = yh_ref[:q, :q]
    packed_ref[q:, :3*q] = yh_ref[2*q:3*q, :3*q]
    packed_ref[q:, 3*q:] = yh_ref[q:2*q, :2*q]
def chol_inverse(gram_sum, rows_summed):
    n = gram_sum.shape[0]
    return pl.pallas_call(
        functools.partial(chol_kernel, rows_summed),
        out_shape=[jax.ShapeDtypeStruct((n, n), jnp.bfloat16)]*2 + [jax.ShapeDtypeStruct((n//2, 5*n//4), jnp.bfloat16)],
        in_specs=[pl.BlockSpec(memory_space=pltpu.VMEM)],
        out_specs=[pl.BlockSpec(memory_space=pltpu.VMEM)]*3,
        scratch_shapes=[pltpu.VMEM((n,n),jnp.bfloat16)]*2+[pltpu.VMEM((NB,NB),jnp.float32)]*2+[pltpu.VMEM((n,NB),jnp.float32),pltpu.VMEM((NB,n),jnp.float32)],
        name="chol_inverse",
        cost_estimate=pl.CostEstimate(flops=6*10**10, transcendentals=0, bytes_accessed=10*2**20),
        compiler_params=pltpu.CompilerParams(vmem_limit_bytes=28 * 1024 * 1024),
    )(gram_sum)


TN = (((0,), (0,)), ((), ()))
MIB = 1024 * 1024


def f32_dot(a, b, dims=NN):
    return lax.dot_general(a, b, dims, preferred_element_type=jnp.float32)


def in_vmem():
    return pl.BlockSpec(memory_space=pltpu.VMEM)


def in_place():
    return pl.BlockSpec(memory_space=pl.ANY)


def in_smem():
    return pl.BlockSpec(memory_space=pltpu.SMEM)


def limit(mib):
    return pltpu.CompilerParams(vmem_limit_bytes=mib * MIB)


def cost(gflop, mib):
    return pl.CostEstimate(flops=gflop * 10**9, transcendentals=0, bytes_accessed=mib * MIB)


def mix(gate_ref, a_ref, b_ref, th_ref):
    rows = a_ref.shape[0] // 2
    half = b_ref.shape[1] // 2
    width = 256
    for c in range(0, half, width):
        p = [f32_dot(a_ref[...], b_ref[:, v * half + c : v * half + c + width]) for v in range(2)]
        for s in range(2):
            for t in range(2):
                mixed = None
                for u in range(2):
                    for v in range(2):
                        term = gate_ref[2 * s + t, 2 * u + v] * p[v][u * rows : (u + 1) * rows]
                        mixed = term if mixed is None else mixed + term
                th_ref[s * rows : (s + 1) * rows, t * half + c : t * half + c + width] = mixed.astype(
                    jnp.bfloat16
                )


def sketch_of(th_ref, om_ref, s_ref):
    for k in range(0, om_ref.shape[1], 256):
        s_ref[:, k : k + 256] = f32_dot(th_ref[...], om_ref[:, k : k + 256]).astype(jnp.bfloat16)


def gram_of(s_refs, g_ref, add):
    for k in range(0, g_ref.shape[0], 256):
        total = None
        for s_ref in s_refs:
            part = f32_dot(s_ref[:, k:], s_ref[:, k : k + 256], TN)
            total = part if total is None else total + part
        if add:
            total = g_ref[k:, k : k + 256] + total
        g_ref[k:, k : k + 256] = total


def theta_kernel(parts, gate_ref, b_ref, *refs):
    for a_ref, th_ref in zip(refs[:parts], refs[parts:]):
        mix(gate_ref, a_ref, b_ref, th_ref)


def theta_of(gate, b_full, blocks):
    parts = len(blocks)
    return pl.pallas_call(
        functools.partial(theta_kernel, parts),
        out_shape=[jax.ShapeDtypeStruct((a.shape[0], b_full.shape[1]), jnp.bfloat16) for a in blocks],
        in_specs=[in_smem()] + [in_vmem()] * (1 + parts),
        out_specs=[in_vmem()] * parts,
        name="theta_of",
        cost_estimate=cost(3 * parts, 4 + 3 * parts),
        compiler_params=limit(28),
    )(gate, b_full, *blocks)


def gram_kernel(parts, om_ref, *refs):
    s_refs = refs[parts : 2 * parts]
    for th_ref, s_ref in zip(refs[:parts], s_refs):
        sketch_of(th_ref, om_ref, s_ref)
    gram_of(s_refs, refs[2 * parts], False)


def sketch_gram(om, thetas):
    parts = len(thetas)
    kept = om.shape[1]
    out = pl.pallas_call(
        functools.partial(gram_kernel, parts),
        out_shape=[jax.ShapeDtypeStruct((th.shape[0], kept), jnp.bfloat16) for th in thetas]
        + [jax.ShapeDtypeStruct((kept, kept), jnp.float32)],
        in_specs=[in_vmem()] * (1 + parts),
        out_specs=[in_vmem()] * (parts + 1),
        name="sketch_gram",
        cost_estimate=cost(4 * parts, 8 + 3 * parts),
        compiler_params=limit(28),
    )(om, *thetas)
    return out[:parts], out[parts]


def last_kernel(gate_ref, b_ref, om_ref, a_ref, gin_ref, th_ref, s_ref, g_ref):
    mix(gate_ref, a_ref, b_ref, th_ref)
    sketch_of(th_ref, om_ref, s_ref)
    gram_of([s_ref], g_ref, True)


def last_chunk(gate, b_full, om, block, gram):
    return pl.pallas_call(
        last_kernel,
        out_shape=[
            jax.ShapeDtypeStruct((block.shape[0], b_full.shape[1]), jnp.bfloat16),
            jax.ShapeDtypeStruct((block.shape[0], om.shape[1]), jnp.bfloat16),
            jax.ShapeDtypeStruct(gram.shape, jnp.float32),
        ],
        in_specs=[in_smem()] + [in_vmem()] * 4,
        out_specs=[in_vmem()] * 3,
        input_output_aliases={4: 2},
        name="last_chunk",
        cost_estimate=cost(7, 20),
        compiler_params=limit(28),
    )(gate, b_full, om, block, gram)


def project_kernel(offsets, right_scale, pair_scale, *refs):
    row_ref, yh_ref, yl_ref = refs[:3]
    s_refs, th_refs, next_refs = refs[3:7], refs[7:11], refs[11:15]
    left_ref, right_ref, mid_h, mid_l, basis_ref, wide_ref = refs[15:21]
    row = row_ref[0]
    rows = s_refs[0].shape[0] // 2
    kept = yh_ref.shape[0]
    mine = pl.ds(pl.multiple_of(row * rows, rows), rows)
    for j in range(4):
        basis_ref[j] = (
            f32_dot(s_refs[j][...], yh_ref[mine, :], NT) + f32_dot(s_refs[j][...], yl_ref[mine, :], NT)
        ).astype(jnp.bfloat16)
    width = right_ref.shape[1]
    for c in range(0, width, 256):
        total = None
        for j in range(4):
            term = f32_dot(basis_ref[j], th_refs[j][:, c : c + 256], TN)
            total = term if total is None else total + term
        right_ref[:, c : c + 256] = (total * right_scale).astype(jnp.bfloat16)
    for t in range(2):
        parts = []
        for d in offsets:
            first = t * (width // 2) + lax.rem(row + d, 4) * rows
            parts.append(pl.ds(pl.multiple_of(first, rows), rows))
        for s in range(2):
            for c in range(0, kept, 256):
                total = None
                for j in range(4):
                    term = f32_dot(
                        right_ref[:, parts[j]], next_refs[j][s * rows : (s + 1) * rows, c : c + 256]
                    )
                    total = term if total is None else total + term
                total = total * pair_scale
                for i in range(2):
                    block = (s * kept + c) // NB + i
                    wide_ref[block, pl.ds(t, rows, stride=2), :] = total[:, i * NB : (i + 1) * NB]
    for c in range(2 * kept // NB):
        high, low = hi_lo(wide_ref[c])
        mid_h[:, c * NB : (c + 1) * NB] = high
        mid_l[:, c * NB : (c + 1) * NB] = low
    for c in range(0, kept, 256):
        left = f32_dot(s_refs[0][:, : c + 256], yh_ref[c : c + 256, : c + 256], NT) + f32_dot(
            s_refs[0][:, : c + 256], yl_ref[c : c + 256, : c + 256], NT
        )
        for i in range(2):
            block = c // NB + i
            for s in range(2):
                wide_ref[block, pl.ds(s, rows, stride=2), :] = left[
                    s * rows : (s + 1) * rows, i * NB : (i + 1) * NB
                ]
            left_ref[:, block * NB : (block + 1) * NB] = wide_ref[block].astype(jnp.bfloat16)


def project(row, yh, yl, sketches, thetas, next_sketches, offsets):
    rows, kept = sketches[0].shape
    width = thetas[0].shape[1]
    return pl.pallas_call(
        functools.partial(
            project_kernel, offsets, 1.0 / math.sqrt(1.0 * width), 1.0 / math.sqrt(0.5 * width)
        ),
        out_shape=[
            jax.ShapeDtypeStruct((rows, kept), jnp.bfloat16),
            jax.ShapeDtypeStruct((rows // 2, width), jnp.bfloat16),
            jax.ShapeDtypeStruct((rows, 2 * kept), jnp.bfloat16),
            jax.ShapeDtypeStruct((rows, 2 * kept), jnp.bfloat16),
        ],
        in_specs=[in_smem()] + [in_vmem()] * 14,
        out_specs=[in_vmem()] * 4,
        scratch_shapes=[
            pltpu.VMEM((4, rows, rows // 2), jnp.bfloat16),
            pltpu.VMEM((2 * kept // NB, rows, NB), jnp.float32),
        ],
        name="project",
        cost_estimate=cost(9, 22),
        compiler_params=limit(40),
    )(row.reshape(1).astype(jnp.int32), yh, yl, *sketches, *thetas, *next_sketches)


def pair_kernel(mid_h, mid_l, packed, odd_ref):
    kept = packed.shape[1] * 4 // 5
    q = kept // 4
    corner = {0: (0, kept), 1: (q, 3 * q), 2: (q, 0), 3: (0, 0)}
    for i in range(4):
        r0, c0 = corner[i]
        depth = (i + 1) * q
        for s in range(2):
            inv = packed[r0 : r0 + q, c0 : c0 + depth]
            out = f32_dot(mid_h[:, s * kept : s * kept + depth], inv, NT)
            out = out + f32_dot(mid_l[:, s * kept : s * kept + depth], inv, NT)
            odd_ref[:, s * kept + i * q : s * kept + (i + 1) * q] = out.astype(jnp.bfloat16)


def odd_product(mid_h, mid_l, packed):
    return pl.pallas_call(
        pair_kernel,
        out_shape=jax.ShapeDtypeStruct(mid_h.shape, jnp.bfloat16),
        in_specs=[in_vmem()] * 3,
        out_specs=in_vmem(),
        name="odd_product",
        cost_estimate=cost(3, 7),
        compiler_params=limit(16),
    )(mid_h, mid_l, packed)


def rot(block, axis, distance):
    count = lax.axis_size(axis)
    return lax.ppermute(block, axis, [(i, (i + distance) % count) for i in range(count)])


def from_behind(block):
    count = lax.axis_size(BOND)
    return lax.ppermute(block, BOND, [(i + 1, i) for i in range(count - 1)])


def place(whole, block, index, dim):
    starts = [0] * whole.ndim
    starts[dim] = index
    return lax.dynamic_update_slice(whole, block, tuple(starts))


def paired(block, axis, bit, dim):
    count = lax.axis_size(axis)
    other = lax.ppermute(block, axis, [(i, i ^ bit) for i in range(count)])
    low = (lax.axis_index(axis) & bit) == 0
    return jnp.stack([jnp.where(low, block, other), jnp.where(low, other, block)], axis=dim)


def shards(left_site, right_site, gate, omega):
    row_count, bond_width = left_site.shape
    own = right_site.shape[0]
    half = own // 2
    n_row = lax.axis_size("row")
    row = lax.axis_index("row")
    tie = lax.optimization_barrier

    bl, br = rot(right_site, "row", 1), rot(right_site, "row", -1)
    om_rows, kept = omega.shape
    n_x, n_z = lax.axis_size("bond_1"), lax.axis_size("bond_0")
    x = lax.axis_index("bond_1")
    strip = paired(paired(omega, "row", 1, 0), "row", 2, 0).reshape(4 * om_rows, kept)
    a0 = left_site.reshape(own, 2, bond_width).transpose(1, 0, 2).reshape(row_count, bond_width)
    strip = paired(paired(strip, "bond_0", 4, 0), "bond_0", 2, 1)
    strip, bl, br, a0 = tie((strip, bl, br, a0))
    bo1, bo2 = rot(bl[:half], "row", 1), rot(br[half:], "row", -1)
    al, ar = rot(a0, "row", 1), rot(a0, "row", -1)
    by_z = paired(strip, "bond_0", 1, 2).reshape(n_z, 4 * om_rows, kept)
    left, right = rot(by_z, "bond_1", 1), rot(by_z, "bond_1", -1)
    b_full = jnp.zeros((n_row * own, right_site.shape[1]), right_site.dtype)
    b_full = place(b_full, right_site, row * own, 0)
    b_full = place(b_full, bl, (row - 1) % n_row * own, 0)
    b_full = place(b_full, br, (row + 1) % n_row * own, 0)
    left, right, bo1, bo2 = tie((left, right, bo1, bo2))
    far_a = rot(left[: n_z // 2], "bond_1", 1)
    far_b = rot(right[n_z // 2 :], "bond_1", -1)
    b_full = place(b_full, bo1, (row + 2) % n_row * own, 0)
    b_full = place(b_full, bo2, (row + 2) % n_row * own + half, 0)
    mine = jnp.zeros((n_z, n_x, 4 * om_rows, kept), omega.dtype)
    for block, d in ((by_z, 0), (left, 1), (right, -1)):
        mine = place(mine, block[:, None], (x - d) % n_x, 1)
    th0 = theta_of(gate, b_full, [a0])
    far_a, far_b, th0, al, ar = tie((far_a, far_b, th0, al, ar))
    ao1, ao2 = rot(al[:own], "row", 1), rot(ar[own:], "row", -1)
    mine = lax.dynamic_update_slice(mine, far_a[:, None], (0, (x + 2) % n_x, 0, 0))
    mine = lax.dynamic_update_slice(mine, far_b[:, None], (n_z // 2, (x + 2) % n_x, 0, 0))
    om = paired(mine, "bond_2", 1, 2).reshape(-1, kept)
    th1 = theta_of(gate, b_full, [al, ar])
    sk, gram = sketch_gram(om, list(th0) + list(th1))
    gram, ao1, ao2 = tie((gram, ao1, ao2))
    ao = jnp.concatenate([ao1, ao2], axis=0)
    th2, sk2, gram = last_chunk(gate, b_full, om, ao, gram)
    thetas, sketches = list(th0) + list(th1) + [th2], list(sk) + [sk2]
    next_sketches = [from_behind(block) for block in sketches]
    yh, yl, packed = chol_inverse(gram, 2.0 * bond_width)
    next_packed = from_behind(packed)
    left_new, right_new, mid_h, mid_l = project(
        row, yh, yl, sketches, thetas, next_sketches, (0, 3, 1, 2)
    )
    odd_pair = odd_product(mid_h, mid_l, next_packed)
    return (left_new, right_new, odd_pair)


def solution(mesh):
    torus = Mesh(
        mesh.devices.reshape(8, 4, 2, mesh.shape["row"]), ("bond_0", "bond_1", "bond_2", "row")
    )
    in_specs = (P(BOND_ROW, None), P(BOND_ROW, None), P(), P(BOND_ROW, None))
    out_specs = (P(BOND_ROW, None), P(BOND_ROW, None), P(BOND_ROW, None))
    return jax.shard_map(
        shards, mesh=torus, in_specs=in_specs, out_specs=out_specs, check_vma=False
    )
```

```python
import functools
import math

import jax
import jax.numpy as jnp
from jax import lax
from jax.experimental import pallas as pl
from jax.experimental.pallas import tpu as pltpu
from jax.sharding import Mesh
from jax.sharding import PartitionSpec as P

BOND_ROW = ("bond_0", "bond_1", "bond_2", "row")
BOND = ("bond_0", "bond_1", "bond_2")
NB = 128


def sub_row(x, c):
    return jnp.broadcast_to(x[c:c+1, :], x.shape)
def lane_col(x, c):
    return jnp.broadcast_to(x[:, c:c+1], x.shape)
def diag_inverse(block):
    groups = NB // 8
    sub = lax.broadcasted_iota(jnp.int32, (8, NB), 0)
    lane = lax.broadcasted_iota(jnp.int32, (8, NB), 1)
    rows = [block[8*r:8*r+8, :] for r in range(groups)]
    er = [jnp.where(lane == sub + 8*r, 1.0, 0.0).astype(jnp.float32) for r in range(groups)]
    out = []
    for p in range(groups):
        cols = [lane_col(rows[p], 8*p+c) for c in range(8)]
        ahead = {r: [lane_col(rows[r], 8*p+c) for c in range(8)] for r in range(p+1, groups)}
        R, E = rows[p], er[p]
        raw = E; pv = cols[0]
        for c in range(0, 8, 2):
            k0, k1 = cols[c], cols[c+1]
            h0 = sub == c; h1 = sub == c+1; hh = h0 | h1
            p00 = sub_row(k0, c); p10 = sub_row(k0, c+1); p11 = sub_row(k1, c+1)
            det = p00*p11 - p10*p10
            r0 = 1.0 / (p00*det)
            rdet = r0*p00
            rp = r0*det
            i00 = p11*rdet; i01 = -p10*rdet; i11 = p00*rdet
            f = p10*rp
            m0 = jnp.where(hh, jnp.where(h0, -i00, -i01), k0*i00 + k1*i01)
            m1 = jnp.where(hh, jnp.where(h0, -i01, -i11), k0*i01 + k1*i11)
            pv = jnp.where(h0, p00, jnp.where(h1, det*rp, pv))
            e0, e1 = sub_row(E, c), sub_row(E, c+1)
            raw = jnp.where(h0, e0, jnp.where(h1, e1 - f*e0, raw))
            if p + 1 < groups:
                R = jnp.where(hh, 0.0, R) - m0*sub_row(R, c) - m1*sub_row(R, c+1)
            E = jnp.where(hh, 0.0, E) - m0*e0 - m1*e1
            for k in range(c+2, 8):
                q = cols[k]
                cols[k] = jnp.where(hh, 0.0, q) - m0*sub_row(q, c) - m1*sub_row(q, c+1)
        out.append(raw * lax.rsqrt(pv))
        if p + 1 < groups:
            rb = [sub_row(R, c) for c in range(8)]; eb = [sub_row(E, c) for c in range(8)]
            for r in range(p+1, groups):
                a, e = rows[r], er[r]
                for c in range(8):
                    a = a - ahead[r][c]*rb[c]
                    e = e - ahead[r][c]*eb[c]
                rows[r], er[r] = a, e
    return jnp.concatenate(out, axis=0)
def hi_lo(x):
    hi = x.astype(jnp.bfloat16)
    return hi, (x - hi.astype(jnp.float32)).astype(jnp.bfloat16)
NT = (((1,), (1,)), ((), ()))
NN = (((1,), (0,)), ((), ()))
def mm3(ah, al, bh, bl, dims):
    d = functools.partial(lax.dot_general, dimension_numbers=dims, preferred_element_type=jnp.float32)
    return d(ah, bh) + (d(ah, bl) + d(al, bh))
def chol_kernel(rows_summed, g_ref, yh_ref, yl_ref, packed_ref, lh, ll, d_ref, inv_ref, cpre, epre):
    n = g_ref.shape[0]
    nblk = n // NB
    i0 = lax.broadcasted_iota(jnp.int32, (NB, NB), 0)
    i1 = lax.broadcasted_iota(jnp.int32, (NB, NB), 1)
    eye = jnp.where(i0 == i1, 1.0, 0.0).astype(jnp.float32)
    tot = jnp.zeros((NB, NB), jnp.float32)
    for b in range(nblk):
        tot = tot + g_ref[b*NB:(b+1)*NB, b*NB:(b+1)*NB]*eye
    trace = jnp.sum(tot)
    tv = jnp.full((8, NB), trace)
    alpha = (n / tv)[0:1, :]
    scale = lax.rsqrt(tv * (1.0/(rows_summed*n)))[0:1, :]
    lh[...] = jnp.zeros_like(lh); ll[...] = jnp.zeros_like(ll)
    yh_ref[...] = jnp.zeros_like(yh_ref); yl_ref[...] = jnp.zeros_like(yl_ref)
    d_ref[...] = g_ref[0:NB, 0:NB]*alpha + 0.01*eye
    cpre[...] = jnp.zeros_like(cpre)
    epre[...] = jnp.zeros_like(epre)
    inv_ref[...] = jnp.zeros_like(inv_ref)
    rowid = lax.broadcasted_iota(jnp.int32, (n, NB), 0)
    def finish(b, depth):
        prev = pl.multiple_of(b*NB, NB)
        ih, il = hi_lo(inv_ref[...])
        epre[:, pl.ds(prev, NB)] = eye*scale
        eh, el = hi_lo(epre[:, :depth])
        yh, yl = hi_lo(mm3(ih, il, eh, el, NN))
        yh_ref[pl.ds(prev, NB), :depth] = yh
        yl_ref[pl.ds(prev, NB), :depth] = yl
        return ih, il, prev
    def body(low, depth, b, carry):
        block = d_ref[...]
        inv = diag_inverse(block)
        prevb = jnp.maximum(b-1, 0)
        ih, il, prev = finish(prevb, depth)
        ch, cl = hi_lo(cpre[low:, :])
        panel = jnp.where(rowid[low:] >= b*NB, mm3(ch, cl, ih, il, NT), 0.0)
        ph, plo = hi_lo(panel)
        lh[low:, pl.ds(prev, NB)] = ph
        ll[low:, pl.ds(prev, NB)] = plo
        cur = pl.multiple_of(b*NB, NB)
        rh, rl = lh[pl.ds(cur, NB), :depth], ll[pl.ds(cur, NB), :depth]
        cpre[low:, :] = g_ref[low:, pl.ds(cur, NB)]*alpha - mm3(lh[low:, :depth], ll[low:, :depth], rh, rl, NT)
        epre[:, :depth] = -mm3(rh, rl, yh_ref[:depth, :depth], yl_ref[:depth, :depth], NN)
        nxt = pl.multiple_of(jnp.minimum(b+1, nblk-1)*NB, NB)
        nh, nl = lh[pl.ds(nxt, NB), :depth], ll[pl.ds(nxt, NB), :depth]
        dpre = g_ref[pl.ds(nxt, NB), pl.ds(nxt, NB)]*alpha + 0.01*eye - mm3(nh, nl, nh, nl, NT)
        inv_ref[...] = inv
        vh, vl = hi_lo(inv)
        xh, xl = hi_lo(cpre[pl.ds(nxt, NB), :])
        th, tl = hi_lo(mm3(xh, xl, vh, vl, NT))
        d_ref[...] = dpre - mm3(th, tl, th, tl, NT)
        return carry
    per = nblk // 2
    for seg in range(2):
        lax.fori_loop(seg*per, (seg+1)*per, functools.partial(body, seg*per*NB, (seg+1)*per*NB), 0)
    finish(nblk-1, n)
    q = n // 4
    packed_ref[:q, :n] = yh_ref[3*q:, :]
    packed_ref[:q, n:] = yh_ref[:q, :q]
    packed_ref[q:, :3*q] = yh_ref[2*q:3*q, :3*q]
    packed_ref[q:, 3*q:] = yh_ref[q:2*q, :2*q]
def chol_inverse(gram_sum, rows_summed):
    n = gram_sum.shape[0]
    return pl.pallas_call(
        functools.partial(chol_kernel, rows_summed),
        out_shape=[jax.ShapeDtypeStruct((n, n), jnp.bfloat16)]*2 + [jax.ShapeDtypeStruct((n//2, 5*n//4), jnp.bfloat16)],
        in_specs=[pl.BlockSpec(memory_space=pltpu.VMEM)],
        out_specs=[pl.BlockSpec(memory_space=pltpu.VMEM)]*3,
        scratch_shapes=[pltpu.VMEM((n,n),jnp.bfloat16)]*2+[pltpu.VMEM((NB,NB),jnp.float32)]*2+[pltpu.VMEM((n,NB),jnp.float32),pltpu.VMEM((NB,n),jnp.float32)],
        name="chol_inverse",
        cost_estimate=pl.CostEstimate(flops=6*10**10, transcendentals=0, bytes_accessed=10*2**20),
        compiler_params=pltpu.CompilerParams(vmem_limit_bytes=18 * 1024 * 1024),
    )(gram_sum)


TN = (((0,), (0,)), ((), ()))
MIB = 1024 * 1024


def f32_dot(a, b, dims=NN):
    return lax.dot_general(a, b, dims, preferred_element_type=jnp.float32)


def in_vmem():
    return pl.BlockSpec(memory_space=pltpu.VMEM)


def in_place():
    return pl.BlockSpec(memory_space=pl.ANY)


def in_smem():
    return pl.BlockSpec(memory_space=pltpu.SMEM)


def limit(mib):
    return pltpu.CompilerParams(vmem_limit_bytes=mib * MIB)


def cost(gflop, mib):
    return pl.CostEstimate(flops=gflop * 10**9, transcendentals=0, bytes_accessed=mib * MIB)


def mix(gate_ref, spins, b_ref, th_ref, first):
    half = b_ref.shape[1] // 2
    width = 256
    for c in range(0, half, width):
        p = {}
        for v in range(2):
            cols = slice(v * half + c, v * half + c + width)
            for u in range(2):
                p[u, v] = f32_dot(spins(u), b_ref[:, cols])
        rows = p[0, 0].shape[0]
        for s in range(2):
            for t in range(2):
                mixed = None
                for u in range(2):
                    for v in range(2):
                        term = gate_ref[2 * s + t, 2 * u + v] * p[u, v]
                        mixed = term if mixed is None else mixed + term
                r = first + s * rows
                th_ref[r : r + rows, t * half + c : t * half + c + width] = mixed.astype(jnp.bfloat16)


def sketch_of(th_ref, om_ref, s_ref):
    for k in range(0, om_ref.shape[1], 256):
        s_ref[:, k : k + 256] = f32_dot(th_ref[...], om_ref[:, k : k + 256]).astype(jnp.bfloat16)


def gram_of(s_refs, g_ref, add):
    for k in range(0, g_ref.shape[0], 256):
        total = None
        for s_ref in s_refs:
            part = f32_dot(s_ref[:, k:], s_ref[:, k : k + 256], TN)
            total = part if total is None else total + part
        if add:
            total = g_ref[k:, k : k + 256] + total
        g_ref[k:, k : k + 256] = total


def theta_kernel(starts, rows, gate_ref, b_ref, *refs):
    depth = b_ref.shape[0]
    for j, (a_ref, r) in enumerate(zip(refs[:-1], starts)):
        mix(
            gate_ref,
            lambda u: a_ref[r : r + rows, u * depth : (u + 1) * depth],
            b_ref,
            refs[-1],
            2 * j * rows,
        )


def theta_of(gate, b_full, blocks, starts, rows):
    return pl.pallas_call(
        functools.partial(theta_kernel, starts, rows),
        out_shape=jax.ShapeDtypeStruct((2 * rows * len(blocks), b_full.shape[1]), jnp.bfloat16),
        in_specs=[in_smem()] + [in_vmem()] * (1 + len(blocks)),
        out_specs=in_vmem(),
        name="theta_of",
        cost_estimate=cost(9, 14),
        compiler_params=limit(18),
    )(gate, b_full, *blocks)


def gram_kernel(om_ref, *refs):
    th_refs, s_ref, g_ref = refs[:-2], refs[-2], refs[-1]
    first = 0
    for th_ref in th_refs:
        for k in range(0, om_ref.shape[1], 256):
            s_ref[first : first + th_ref.shape[0], k : k + 256] = f32_dot(
                th_ref[...], om_ref[:, k : k + 256]
            ).astype(jnp.bfloat16)
        first += th_ref.shape[0]
    gram_of([s_ref], g_ref, False)


def sketch_gram(om, thetas):
    rows = sum(th.shape[0] for th in thetas)
    kept = om.shape[1]
    return pl.pallas_call(
        gram_kernel,
        out_shape=[
            jax.ShapeDtypeStruct((rows, kept), jnp.bfloat16),
            jax.ShapeDtypeStruct((kept, kept), jnp.float32),
        ],
        in_specs=[in_vmem()] * (1 + len(thetas)),
        out_specs=[in_vmem()] * 2,
        name="sketch_gram",
        cost_estimate=cost(10, 17),
        compiler_params=limit(20),
    )(om, *thetas)


def last_kernel(gate_ref, b_ref, om_ref, a0_ref, a1_ref, gin_ref, th_ref, s_ref, g_ref):
    depth = b_ref.shape[0]

    def spins(u):
        cols = slice(u * depth, (u + 1) * depth)
        return jnp.concatenate([a0_ref[:, cols], a1_ref[:, cols]], axis=0)

    mix(gate_ref, spins, b_ref, th_ref, 0)
    sketch_of(th_ref, om_ref, s_ref)
    gram_of([s_ref], g_ref, True)


def last_chunk(gate, b_full, om, halves, gram):
    rows = 4 * halves[0].shape[0]
    return pl.pallas_call(
        last_kernel,
        out_shape=[
            jax.ShapeDtypeStruct((rows, b_full.shape[1]), jnp.bfloat16),
            jax.ShapeDtypeStruct((rows, om.shape[1]), jnp.bfloat16),
            jax.ShapeDtypeStruct(gram.shape, jnp.float32),
        ],
        in_specs=[in_smem()] + [in_vmem()] * 5,
        out_specs=[in_vmem()] * 3,
        input_output_aliases={5: 2},
        name="last_chunk",
        cost_estimate=cost(7, 20),
        compiler_params=limit(24),
    )(gate, b_full, om, *halves, gram)


def project_kernel(offsets, right_scale, pair_scale, *refs):
    row_ref, yh_ref, yl_ref = refs[:3]
    s_refs, th_hbm, next_refs = refs[3:5], refs[5:8], refs[8:10]
    left_ref, right_ref, mid_h, mid_l, basis_ref, wide_ref, th_ref, sems = refs[10:18]
    row = row_ref[0]
    kept = yh_ref.shape[0]
    rows = right_ref.shape[0]
    copies = []
    first = 0
    for i, src in enumerate(th_hbm):
        dst = th_ref.at[pl.ds(first, src.shape[0]), :]
        copies.append(pltpu.make_async_copy(src, dst, sems.at[i]))
        copies[-1].start()
        first += src.shape[0]
    mine = pl.ds(pl.multiple_of(row * rows, rows), rows)
    first = 0
    for s_ref in s_refs:
        count = s_ref.shape[0]
        basis_ref[first : first + count, :] = (
            f32_dot(s_ref[...], yh_ref[mine, :], NT) + f32_dot(s_ref[...], yl_ref[mine, :], NT)
        ).astype(jnp.bfloat16)
        first += count
    for c in range(0, kept, 256):
        own = slice(0, 2 * rows)
        left = f32_dot(s_refs[0][own, : c + 256], yh_ref[c : c + 256, : c + 256], NT) + f32_dot(
            s_refs[0][own, : c + 256], yl_ref[c : c + 256, : c + 256], NT
        )
        for i in range(2):
            block = c // NB + i
            for s in range(2):
                wide_ref[block, pl.ds(s, rows, stride=2), :] = left[
                    s * rows : (s + 1) * rows, i * NB : (i + 1) * NB
                ]
            left_ref[:, block * NB : (block + 1) * NB] = wide_ref[block].astype(jnp.bfloat16)
    for copy in copies:
        copy.wait()
    width = right_ref.shape[1]
    for c in range(0, width, 256):
        total = f32_dot(basis_ref[...], th_ref[:, c : c + 256], TN)
        right_ref[:, c : c + 256] = (total * right_scale).astype(jnp.bfloat16)
    for t in range(2):
        parts = []
        for d in offsets:
            start = t * (width // 2) + lax.rem(row + d, 4) * rows
            parts.append(pl.ds(pl.multiple_of(start, rows), rows))
        for s in range(2):
            for c in range(0, kept, 256):
                total = None
                for j in range(4):
                    if j < 3:
                        r, src = (2 * j + s) * rows, next_refs[0]
                    else:
                        r, src = s * rows, next_refs[1]
                    term = f32_dot(right_ref[:, parts[j]], src[r : r + rows, c : c + 256])
                    total = term if total is None else total + term
                total = total * pair_scale
                for i in range(2):
                    block = (s * kept + c) // NB + i
                    wide_ref[block, pl.ds(t, rows, stride=2), :] = total[:, i * NB : (i + 1) * NB]
    for c in range(2 * kept // NB):
        high, low = hi_lo(wide_ref[c])
        mid_h[:, c * NB : (c + 1) * NB] = high
        mid_l[:, c * NB : (c + 1) * NB] = low


def project(row, yh, yl, sketches, thetas, next_sketches, offsets):
    rows, kept = sketches[1].shape
    width = thetas[0].shape[1]
    total_rows = sum(th.shape[0] for th in thetas)
    return pl.pallas_call(
        functools.partial(
            project_kernel, offsets, 1.0 / math.sqrt(1.0 * width), 1.0 / math.sqrt(0.5 * width)
        ),
        out_shape=[
            jax.ShapeDtypeStruct((rows, kept), jnp.bfloat16),
            jax.ShapeDtypeStruct((rows // 2, width), jnp.bfloat16),
            jax.ShapeDtypeStruct((rows, 2 * kept), jnp.bfloat16),
            jax.ShapeDtypeStruct((rows, 2 * kept), jnp.bfloat16),
        ],
        in_specs=[in_smem()] + [in_vmem()] * 4 + [in_place()] * 3 + [in_vmem()] * 2,
        out_specs=[in_vmem()] * 4,
        scratch_shapes=[
            pltpu.VMEM((total_rows, rows // 2), jnp.bfloat16),
            pltpu.VMEM((2 * kept // NB, rows, NB), jnp.float32),
            pltpu.VMEM((total_rows, width), jnp.bfloat16),
            pltpu.SemaphoreType.DMA((3,)),
        ],
        name="project",
        cost_estimate=cost(9, 22),
        compiler_params=limit(34),
    )(row.reshape(1).astype(jnp.int32), yh, yl, *sketches, *thetas, *next_sketches)


def pair_kernel(mid_h, mid_l, packed, odd_ref):
    kept = packed.shape[1] * 4 // 5
    q = kept // 4
    corner = {0: (0, kept), 1: (q, 3 * q), 2: (q, 0), 3: (0, 0)}
    for i in range(4):
        r0, c0 = corner[i]
        depth = (i + 1) * q
        for s in range(2):
            inv = packed[r0 : r0 + q, c0 : c0 + depth]
            out = f32_dot(mid_h[:, s * kept : s * kept + depth], inv, NT)
            out = out + f32_dot(mid_l[:, s * kept : s * kept + depth], inv, NT)
            odd_ref[:, s * kept + i * q : s * kept + (i + 1) * q] = out.astype(jnp.bfloat16)


def odd_product(mid_h, mid_l, packed):
    return pl.pallas_call(
        pair_kernel,
        out_shape=jax.ShapeDtypeStruct(mid_h.shape, jnp.bfloat16),
        in_specs=[in_vmem()] * 3,
        out_specs=in_vmem(),
        name="odd_product",
        cost_estimate=cost(3, 7),
        compiler_params=limit(16),
    )(mid_h, mid_l, packed)


def rot(block, axis, distance):
    count = lax.axis_size(axis)
    return lax.ppermute(block, axis, [(i, (i + distance) % count) for i in range(count)])


def from_behind(block):
    count = lax.axis_size(BOND)
    return lax.ppermute(block, BOND, [(i + 1, i) for i in range(count - 1)])


def place(whole, block, index, dim):
    starts = [0] * whole.ndim
    starts[dim] = index
    return lax.dynamic_update_slice(whole, block, tuple(starts))


def paired(block, axis, bit, dim):
    count = lax.axis_size(axis)
    other = lax.ppermute(block, axis, [(i, i ^ bit) for i in range(count)])
    low = (lax.axis_index(axis) & bit) == 0
    return jnp.stack([jnp.where(low, block, other), jnp.where(low, other, block)], axis=dim)


def shards(left_site, right_site, gate, omega):
    row_count, bond_width = left_site.shape
    own = right_site.shape[0]
    half = own // 2
    n_row = lax.axis_size("row")
    row = lax.axis_index("row")
    tie = lax.optimization_barrier
    om_rows, kept = omega.shape
    n_x, n_z = lax.axis_size("bond_1"), lax.axis_size("bond_0")
    x, core = lax.axis_index("bond_1"), lax.axis_index("bond_2")

    bl, br = rot(right_site, "row", 1), rot(right_site, "row", -1)
    strip = paired(paired(omega, "row", 1, 0), "row", 2, 0).reshape(4 * om_rows, kept)
    a0 = left_site.reshape(own, 2 * bond_width)
    strip = paired(paired(strip, "bond_0", 4, 0), "bond_0", 2, 1)
    strip, bl, br, a0 = tie((strip, bl, br, a0))
    b_o0, b_o1 = rot(bl[:half], "row", 1), rot(br[half:], "row", -1)
    al, ar = rot(a0, "row", 1), rot(a0, "row", -1)
    b_full = jnp.zeros((n_row * own, right_site.shape[1]), right_site.dtype)
    b_full = place(b_full, right_site, row * own, 0)
    b_full = place(b_full, bl, (row - 1) % n_row * own, 0)
    b_full = place(b_full, br, (row + 1) % n_row * own, 0)
    by_z = paired(strip, "bond_0", 1, 2).reshape(n_z, 4 * om_rows, kept)
    by_z, b_o0, b_o1 = tie((by_z, b_o0, b_o1))
    left, right = rot(by_z, "bond_1", 1), rot(by_z, "bond_1", -1)
    far_a = rot(left[: n_z // 2], "bond_1", 1)
    far_b = rot(right[n_z // 2 :], "bond_1", -1)
    a_o0, a_o1 = rot(al[:half], "row", 1), rot(ar[half:], "row", -1)
    b_full = place(b_full, b_o0, (row + 2) % n_row * own, 0)
    b_full = place(b_full, b_o1, (row + 2) % n_row * own + half, 0)
    mine = jnp.zeros((n_z, n_x, 4 * om_rows, kept), omega.dtype)
    for block, d in ((by_z, 0), (left, 1), (right, -1)):
        mine = place(mine, block[:, None], (x - d) % n_x, 1)
    mine = lax.dynamic_update_slice(mine, far_a[:, None], (0, (x + 2) % n_x, 0, 0))
    mine = lax.dynamic_update_slice(mine, far_b[:, None], (n_z // 2, (x + 2) % n_x, 0, 0))
    th0 = theta_of(gate, b_full, [a0], (0,), own)
    al, ar, th0 = tie((al, ar, th0))
    other = rot(mine, "bond_2", 1)
    om = jnp.stack([jnp.where(core == 0, mine, other), jnp.where(core == 0, other, mine)], axis=2)
    om = om.reshape(-1, kept)
    th1 = theta_of(gate, b_full, [al, ar], (0, 0), own)
    om, th1 = tie((om, th1))
    sk, gram = sketch_gram(om, [th0, th1])
    gram, a_o0, a_o1 = tie((gram, a_o0, a_o1))
    th2, sk2, gram = last_chunk(gate, b_full, om, [a_o0, a_o1], gram)
    next_sketches = [from_behind(sk), from_behind(sk2)]
    yh, yl, packed = chol_inverse(gram, 2.0 * bond_width)
    next_packed = from_behind(packed)
    left_new, right_new, mid_h, mid_l = project(
        row, yh, yl, [sk, sk2], [th0, th1, th2], next_sketches, (0, 3, 1, 2)
    )
    odd_pair = odd_product(mid_h, mid_l, next_packed)
    return (left_new, right_new, odd_pair)


def solution(mesh):
    torus = Mesh(
        mesh.devices.reshape(8, 4, 2, mesh.shape["row"]), ("bond_0", "bond_1", "bond_2", "row")
    )
    in_specs = (P(BOND_ROW, None), P(BOND_ROW, None), P(), P(BOND_ROW, None))
    out_specs = (P(BOND_ROW, None), P(BOND_ROW, None), P(BOND_ROW, None))
    return jax.shard_map(
        shards, mesh=torus, in_specs=in_specs, out_specs=out_specs, check_vma=False
    )
```

```python
import functools
import math

import jax
import jax.numpy as jnp
from jax import lax
from jax.experimental import pallas as pl
from jax.experimental.pallas import tpu as pltpu
from jax.sharding import Mesh
from jax.sharding import PartitionSpec as P

BOND_ROW = ("bond_0", "bond_1", "bond_2", "row")
BOND = ("bond_0", "bond_1", "bond_2")
NB = 128


def sub_row(x, c):
    return jnp.broadcast_to(x[c:c+1, :], x.shape)
def lane_col(x, c):
    return jnp.broadcast_to(x[:, c:c+1], x.shape)
def diag_inverse(block):
    groups = NB // 8
    sub = lax.broadcasted_iota(jnp.int32, (8, NB), 0)
    lane = lax.broadcasted_iota(jnp.int32, (8, NB), 1)
    rows = [block[8*r:8*r+8, :] for r in range(groups)]
    er = [jnp.where(lane == sub + 8*r, 1.0, 0.0).astype(jnp.float32) for r in range(groups)]
    out = []
    for p in range(groups):
        cols = [lane_col(rows[p], 8*p+c) for c in range(8)]
        ahead = {r: [lane_col(rows[r], 8*p+c) for c in range(8)] for r in range(p+1, groups)}
        R, E = rows[p], er[p]
        raw = E; pv = cols[0]
        for c in range(0, 8, 2):
            k0, k1 = cols[c], cols[c+1]
            h0 = sub == c; h1 = sub == c+1; hh = h0 | h1
            p00 = sub_row(k0, c); p10 = sub_row(k0, c+1); p11 = sub_row(k1, c+1)
            det = p00*p11 - p10*p10
            r0 = 1.0 / (p00*det)
            rdet = r0*p00
            rp = r0*det
            i00 = p11*rdet; i01 = -p10*rdet; i11 = p00*rdet
            f = p10*rp
            m0 = jnp.where(hh, jnp.where(h0, -i00, -i01), k0*i00 + k1*i01)
            m1 = jnp.where(hh, jnp.where(h0, -i01, -i11), k0*i01 + k1*i11)
            pv = jnp.where(h0, p00, jnp.where(h1, det*rp, pv))
            e0, e1 = sub_row(E, c), sub_row(E, c+1)
            raw = jnp.where(h0, e0, jnp.where(h1, e1 - f*e0, raw))
            if p + 1 < groups:
                R = jnp.where(hh, 0.0, R) - m0*sub_row(R, c) - m1*sub_row(R, c+1)
            E = jnp.where(hh, 0.0, E) - m0*e0 - m1*e1
            for k in range(c+2, 8):
                q = cols[k]
                cols[k] = jnp.where(hh, 0.0, q) - m0*sub_row(q, c) - m1*sub_row(q, c+1)
        out.append(raw * lax.rsqrt(pv))
        if p + 1 < groups:
            rb = [sub_row(R, c) for c in range(8)]; eb = [sub_row(E, c) for c in range(8)]
            for r in range(p+1, groups):
                a, e = rows[r], er[r]
                for c in range(8):
                    a = a - ahead[r][c]*rb[c]
                    e = e - ahead[r][c]*eb[c]
                rows[r], er[r] = a, e
    return jnp.concatenate(out, axis=0)
def hi_lo(x):
    hi = x.astype(jnp.bfloat16)
    return hi, (x - hi.astype(jnp.float32)).astype(jnp.bfloat16)
NT = (((1,), (1,)), ((), ()))
NN = (((1,), (0,)), ((), ()))
def mm3(ah, al, bh, bl, dims):
    d = functools.partial(lax.dot_general, dimension_numbers=dims, preferred_element_type=jnp.float32)
    return d(ah, bh) + (d(ah, bl) + d(al, bh))
def chol_kernel(rows_summed, g_ref, yh_ref, yl_ref, packed_ref, lh, ll, d_ref, inv_ref, cpre, epre):
    n = g_ref.shape[0]
    nblk = n // NB
    i0 = lax.broadcasted_iota(jnp.int32, (NB, NB), 0)
    i1 = lax.broadcasted_iota(jnp.int32, (NB, NB), 1)
    eye = jnp.where(i0 == i1, 1.0, 0.0).astype(jnp.float32)
    tot = jnp.zeros((NB, NB), jnp.float32)
    for b in range(nblk):
        tot = tot + g_ref[b*NB:(b+1)*NB, b*NB:(b+1)*NB]*eye
    trace = jnp.sum(tot)
    tv = jnp.full((8, NB), trace)
    alpha = (n / tv)[0:1, :]
    scale = lax.rsqrt(tv * (1.0/(rows_summed*n)))[0:1, :]
    lh[...] = jnp.zeros_like(lh); ll[...] = jnp.zeros_like(ll)
    yh_ref[...] = jnp.zeros_like(yh_ref); yl_ref[...] = jnp.zeros_like(yl_ref)
    d_ref[...] = g_ref[0:NB, 0:NB]*alpha + 0.01*eye
    cpre[...] = jnp.zeros_like(cpre)
    epre[...] = jnp.zeros_like(epre)
    inv_ref[...] = jnp.zeros_like(inv_ref)
    rowid = lax.broadcasted_iota(jnp.int32, (n, NB), 0)
    def finish(b, depth):
        prev = pl.multiple_of(b*NB, NB)
        ih, il = hi_lo(inv_ref[...])
        epre[:, pl.ds(prev, NB)] = eye*scale
        eh, el = hi_lo(epre[:, :depth])
        yh, yl = hi_lo(mm3(ih, il, eh, el, NN))
        yh_ref[pl.ds(prev, NB), :depth] = yh
        yl_ref[pl.ds(prev, NB), :depth] = yl
        return ih, il, prev
    def body(low, depth, b, carry):
        block = d_ref[...]
        inv = diag_inverse(block)
        prevb = jnp.maximum(b-1, 0)
        ih, il, prev = finish(prevb, depth)
        ch, cl = hi_lo(cpre[low:, :])
        panel = jnp.where(rowid[low:] >= b*NB, mm3(ch, cl, ih, il, NT), 0.0)
        ph, plo = hi_lo(panel)
        lh[low:, pl.ds(prev, NB)] = ph
        ll[low:, pl.ds(prev, NB)] = plo
        cur = pl.multiple_of(b*NB, NB)
        rh, rl = lh[pl.ds(cur, NB), :depth], ll[pl.ds(cur, NB), :depth]
        cpre[low:, :] = g_ref[low:, pl.ds(cur, NB)]*alpha - mm3(lh[low:, :depth], ll[low:, :depth], rh, rl, NT)
        epre[:, :depth] = -mm3(rh, rl, yh_ref[:depth, :depth], yl_ref[:depth, :depth], NN)
        nxt = pl.multiple_of(jnp.minimum(b+1, nblk-1)*NB, NB)
        nh, nl = lh[pl.ds(nxt, NB), :depth], ll[pl.ds(nxt, NB), :depth]
        dpre = g_ref[pl.ds(nxt, NB), pl.ds(nxt, NB)]*alpha + 0.01*eye - mm3(nh, nl, nh, nl, NT)
        inv_ref[...] = inv
        vh, vl = hi_lo(inv)
        xh, xl = hi_lo(cpre[pl.ds(nxt, NB), :])
        th, tl = hi_lo(mm3(xh, xl, vh, vl, NT))
        d_ref[...] = dpre - mm3(th, tl, th, tl, NT)
        return carry
    per = nblk // 2
    for seg in range(2):
        lax.fori_loop(seg*per, (seg+1)*per, functools.partial(body, seg*per*NB, (seg+1)*per*NB), 0)
    finish(nblk-1, n)
    q = n // 4
    packed_ref[:q, :n] = yh_ref[3*q:, :]
    packed_ref[:q, n:] = yh_ref[:q, :q]
    packed_ref[q:, :3*q] = yh_ref[2*q:3*q, :3*q]
    packed_ref[q:, 3*q:] = yh_ref[q:2*q, :2*q]
def chol_inverse(gram_sum, rows_summed):
    n = gram_sum.shape[0]
    return pl.pallas_call(
        functools.partial(chol_kernel, rows_summed),
        out_shape=[jax.ShapeDtypeStruct((n, n), jnp.bfloat16)]*2 + [jax.ShapeDtypeStruct((n//2, 5*n//4), jnp.bfloat16)],
        in_specs=[pl.BlockSpec(memory_space=pltpu.VMEM)],
        out_specs=[pl.BlockSpec(memory_space=pltpu.VMEM)]*3,
        scratch_shapes=[pltpu.VMEM((n,n),jnp.bfloat16)]*2+[pltpu.VMEM((NB,NB),jnp.float32)]*2+[pltpu.VMEM((n,NB),jnp.float32),pltpu.VMEM((NB,n),jnp.float32)],
        name="chol_inverse",
        cost_estimate=pl.CostEstimate(flops=6*10**10, transcendentals=0, bytes_accessed=10*2**20),
        compiler_params=pltpu.CompilerParams(vmem_limit_bytes=18 * 1024 * 1024),
    )(gram_sum)


TN = (((0,), (0,)), ((), ()))
MIB = 1024 * 1024


def f32_dot(a, b, dims=NN):
    return lax.dot_general(a, b, dims, preferred_element_type=jnp.float32)


def in_vmem():
    return pl.BlockSpec(memory_space=pltpu.VMEM)


def in_place():
    return pl.BlockSpec(memory_space=pl.ANY)


def in_smem():
    return pl.BlockSpec(memory_space=pltpu.SMEM)


def limit(mib):
    return pltpu.CompilerParams(vmem_limit_bytes=mib * MIB)


def cost(gflop, mib):
    return pl.CostEstimate(flops=gflop * 10**9, transcendentals=0, bytes_accessed=mib * MIB)


def mix(gate_ref, spins, b_ref, th_ref, first):
    half = b_ref.shape[1] // 2
    width = 256
    for c in range(0, half, width):
        p = {}
        for v in range(2):
            cols = slice(v * half + c, v * half + c + width)
            for u in range(2):
                p[u, v] = f32_dot(spins(u), b_ref[:, cols])
        rows = p[0, 0].shape[0]
        for s in range(2):
            for t in range(2):
                mixed = None
                for u in range(2):
                    for v in range(2):
                        term = gate_ref[2 * s + t, 2 * u + v] * p[u, v]
                        mixed = term if mixed is None else mixed + term
                r = first + s * rows
                th_ref[r : r + rows, t * half + c : t * half + c + width] = mixed.astype(jnp.bfloat16)


def sketch_of(th_ref, om_ref, s_ref, first):
    rows = th_ref.shape[0]
    for k in range(0, om_ref.shape[1], 256):
        s_ref[first : first + rows, k : k + 256] = f32_dot(
            th_ref[...], om_ref[:, k : k + 256]
        ).astype(jnp.bfloat16)


def gram_of(s_ref, first, end, g_ref, add):
    for k in range(0, g_ref.shape[0], 256):
        total = f32_dot(s_ref[first:end, k:], s_ref[first:end, k : k + 256], TN)
        if add:
            total = g_ref[k:, k : k + 256] + total
        g_ref[k:, k : k + 256] = total


def theta_kernel(starts, rows, gate_ref, b_ref, *refs):
    depth = b_ref.shape[0]
    for j, (a_ref, r) in enumerate(zip(refs[:-1], starts)):
        mix(
            gate_ref,
            lambda u: a_ref[r : r + rows, u * depth : (u + 1) * depth],
            b_ref,
            refs[-1],
            2 * j * rows,
        )


def theta_of(gate, b_full, blocks, starts, rows):
    return pl.pallas_call(
        functools.partial(theta_kernel, starts, rows),
        out_shape=jax.ShapeDtypeStruct((2 * rows * len(blocks), b_full.shape[1]), jnp.bfloat16),
        in_specs=[in_smem()] + [in_vmem()] * (1 + len(blocks)),
        out_specs=in_vmem(),
        name="theta_of",
        cost_estimate=cost(9, 14),
        compiler_params=limit(18),
    )(gate, b_full, *blocks)


def gram_kernel(om_ref, *refs):
    th_refs, s_ref, g_ref = refs[:-2], refs[-2], refs[-1]
    end = 0
    for th_ref in th_refs:
        sketch_of(th_ref, om_ref, s_ref, end)
        end += th_ref.shape[0]
    gram_of(s_ref, 0, end, g_ref, False)


def sketch_gram(om, thetas, rows):
    kept = om.shape[1]
    return pl.pallas_call(
        gram_kernel,
        out_shape=[
            jax.ShapeDtypeStruct((rows, kept), jnp.bfloat16),
            jax.ShapeDtypeStruct((kept, kept), jnp.float32),
        ],
        in_specs=[in_vmem()] * (1 + len(thetas)),
        out_specs=[in_vmem()] * 2,
        name="sketch_gram",
        cost_estimate=cost(10, 17),
        compiler_params=limit(22),
    )(om, *thetas)


def last_kernel(gate_ref, b_ref, om_ref, a0_ref, a1_ref, sin_ref, gin_ref, th_ref, s_ref, g_ref):
    depth = b_ref.shape[0]

    def spins(u):
        cols = slice(u * depth, (u + 1) * depth)
        return jnp.concatenate([a0_ref[:, cols], a1_ref[:, cols]], axis=0)

    mix(gate_ref, spins, b_ref, th_ref, 0)
    end = s_ref.shape[0]
    first = end - th_ref.shape[0]
    sketch_of(th_ref, om_ref, s_ref, first)
    gram_of(s_ref, first, end, g_ref, True)


def last_chunk(gate, b_full, om, halves, sketch, gram):
    rows = 4 * halves[0].shape[0]
    return pl.pallas_call(
        last_kernel,
        out_shape=[
            jax.ShapeDtypeStruct((rows, b_full.shape[1]), jnp.bfloat16),
            jax.ShapeDtypeStruct(sketch.shape, jnp.bfloat16),
            jax.ShapeDtypeStruct(gram.shape, jnp.float32),
        ],
        in_specs=[in_smem()] + [in_vmem()] * 6,
        out_specs=[in_vmem()] * 3,
        input_output_aliases={5: 1, 6: 2},
        name="last_chunk",
        cost_estimate=cost(7, 20),
        compiler_params=limit(32),
    )(gate, b_full, om, *halves, sketch, gram)


def project_kernel(offsets, right_scale, pair_scale, *refs):
    row_ref, yh_ref, yl_ref, s_ref = refs[:4]
    th_hbm, next_hbm = refs[4:7], refs[7]
    left_ref, right_ref, mid_h, mid_l, basis_ref, wide_ref, th_ref, next_ref, sems = refs[8:17]
    row = row_ref[0]
    kept = yh_ref.shape[0]
    rows = right_ref.shape[0]
    copies = []
    first = 0
    for i, src in enumerate(th_hbm):
        dst = th_ref.at[pl.ds(first, src.shape[0]), :]
        copies.append(pltpu.make_async_copy(src, dst, sems.at[i]))
        copies[-1].start()
        first += src.shape[0]
    next_copy = pltpu.make_async_copy(next_hbm, next_ref, sems.at[3])
    next_copy.start()
    mine = pl.ds(pl.multiple_of(row * rows, rows), rows)
    for first in range(0, s_ref.shape[0], 2 * rows):
        part = slice(first, first + 2 * rows)
        basis_ref[part, :] = (
            f32_dot(s_ref[part, :], yh_ref[mine, :], NT) + f32_dot(s_ref[part, :], yl_ref[mine, :], NT)
        ).astype(jnp.bfloat16)
    for c in range(0, kept, 256):
        own = slice(0, 2 * rows)
        left = f32_dot(s_ref[own, : c + 256], yh_ref[c : c + 256, : c + 256], NT) + f32_dot(
            s_ref[own, : c + 256], yl_ref[c : c + 256, : c + 256], NT
        )
        for i in range(2):
            block = c // NB + i
            for s in range(2):
                wide_ref[block, pl.ds(s, rows, stride=2), :] = left[
                    s * rows : (s + 1) * rows, i * NB : (i + 1) * NB
                ]
            left_ref[:, block * NB : (block + 1) * NB] = wide_ref[block].astype(jnp.bfloat16)
    for copy in copies:
        copy.wait()
    width = right_ref.shape[1]
    for c in range(0, width, 256):
        total = f32_dot(basis_ref[...], th_ref[:, c : c + 256], TN)
        right_ref[:, c : c + 256] = (total * right_scale).astype(jnp.bfloat16)
    next_copy.wait()
    for t in range(2):
        parts = []
        for d in offsets:
            start = t * (width // 2) + lax.rem(row + d, 4) * rows
            parts.append(pl.ds(pl.multiple_of(start, rows), rows))
        for s in range(2):
            for c in range(0, kept, 256):
                total = None
                for j in range(4):
                    r = (2 * j + s) * rows
                    term = f32_dot(right_ref[:, parts[j]], next_ref[r : r + rows, c : c + 256])
                    total = term if total is None else total + term
                total = total * pair_scale
                for i in range(2):
                    block = (s * kept + c) // NB + i
                    wide_ref[block, pl.ds(t, rows, stride=2), :] = total[:, i * NB : (i + 1) * NB]
    for c in range(2 * kept // NB):
        high, low = hi_lo(wide_ref[c])
        mid_h[:, c * NB : (c + 1) * NB] = high
        mid_l[:, c * NB : (c + 1) * NB] = low


def project(row, yh, yl, sketch, thetas, next_sketch, offsets):
    total_rows, kept = sketch.shape
    rows = total_rows // 4
    width = thetas[0].shape[1]
    return pl.pallas_call(
        functools.partial(
            project_kernel, offsets, 1.0 / math.sqrt(1.0 * width), 1.0 / math.sqrt(0.5 * width)
        ),
        out_shape=[
            jax.ShapeDtypeStruct((rows, kept), jnp.bfloat16),
            jax.ShapeDtypeStruct((rows // 2, width), jnp.bfloat16),
            jax.ShapeDtypeStruct((rows, 2 * kept), jnp.bfloat16),
            jax.ShapeDtypeStruct((rows, 2 * kept), jnp.bfloat16),
        ],
        in_specs=[in_smem()] + [in_vmem()] * 3 + [in_place()] * 4,
        out_specs=[in_vmem()] * 4,
        scratch_shapes=[
            pltpu.VMEM((total_rows, rows // 2), jnp.bfloat16),
            pltpu.VMEM((2 * kept // NB, rows, NB), jnp.float32),
            pltpu.VMEM((total_rows, width), jnp.bfloat16),
            pltpu.VMEM((total_rows, kept), jnp.bfloat16),
            pltpu.SemaphoreType.DMA((4,)),
        ],
        name="project",
        cost_estimate=cost(9, 22),
        compiler_params=limit(34),
    )(row.reshape(1).astype(jnp.int32), yh, yl, sketch, *thetas, next_sketch)


def pair_kernel(mid_h, mid_l, packed, odd_ref):
    kept = packed.shape[1] * 4 // 5
    q = kept // 4
    corner = {0: (0, kept), 1: (q, 3 * q), 2: (q, 0), 3: (0, 0)}
    for i in range(4):
        r0, c0 = corner[i]
        depth = (i + 1) * q
        for s in range(2):
            inv = packed[r0 : r0 + q, c0 : c0 + depth]
            out = f32_dot(mid_h[:, s * kept : s * kept + depth], inv, NT)
            out = out + f32_dot(mid_l[:, s * kept : s * kept + depth], inv, NT)
            odd_ref[:, s * kept + i * q : s * kept + (i + 1) * q] = out.astype(jnp.bfloat16)


def odd_product(mid_h, mid_l, packed):
    return pl.pallas_call(
        pair_kernel,
        out_shape=jax.ShapeDtypeStruct(mid_h.shape, jnp.bfloat16),
        in_specs=[in_vmem()] * 3,
        out_specs=in_vmem(),
        name="odd_product",
        cost_estimate=cost(3, 7),
        compiler_params=limit(16),
    )(mid_h, mid_l, packed)


def rot(block, axis, distance):
    count = lax.axis_size(axis)
    return lax.ppermute(block, axis, [(i, (i + distance) % count) for i in range(count)])


def from_behind(block):
    count = lax.axis_size(BOND)
    return lax.ppermute(block, BOND, [(i + 1, i) for i in range(count - 1)])


def place(whole, block, index, dim):
    starts = [0] * whole.ndim
    starts[dim] = index
    return lax.dynamic_update_slice(whole, block, tuple(starts))


def paired(block, axis, bit, dim):
    count = lax.axis_size(axis)
    other = lax.ppermute(block, axis, [(i, i ^ bit) for i in range(count)])
    low = (lax.axis_index(axis) & bit) == 0
    return jnp.stack([jnp.where(low, block, other), jnp.where(low, other, block)], axis=dim)


def shards(left_site, right_site, gate, omega):
    row_count, bond_width = left_site.shape
    own = right_site.shape[0]
    half = own // 2
    n_row = lax.axis_size("row")
    row = lax.axis_index("row")
    tie = lax.optimization_barrier
    om_rows, kept = omega.shape
    n_x, n_z = lax.axis_size("bond_1"), lax.axis_size("bond_0")
    x, core = lax.axis_index("bond_1"), lax.axis_index("bond_2")

    bl, br = rot(right_site, "row", 1), rot(right_site, "row", -1)
    strip = paired(paired(omega, "row", 1, 0), "row", 2, 0).reshape(4 * om_rows, kept)
    a0 = left_site.reshape(own, 2 * bond_width)
    strip = paired(paired(strip, "bond_0", 4, 0), "bond_0", 2, 1)
    strip, bl, br, a0 = tie((strip, bl, br, a0))
    b_o0, b_o1 = rot(bl[:half], "row", 1), rot(br[half:], "row", -1)
    al, ar = rot(a0, "row", 1), rot(a0, "row", -1)
    b_full = jnp.zeros((n_row * own, right_site.shape[1]), right_site.dtype)
    b_full = place(b_full, right_site, row * own, 0)
    b_full = place(b_full, bl, (row - 1) % n_row * own, 0)
    b_full = place(b_full, br, (row + 1) % n_row * own, 0)
    by_z = paired(strip, "bond_0", 1, 2).reshape(n_z, 4 * om_rows, kept)
    by_z, b_o0, b_o1 = tie((by_z, b_o0, b_o1))
    left, right = rot(by_z, "bond_1", 1), rot(by_z, "bond_1", -1)
    far_a = rot(left[: n_z // 2], "bond_1", 1)
    far_b = rot(right[n_z // 2 :], "bond_1", -1)
    a_o0, a_o1 = rot(al[:half], "row", 1), rot(ar[half:], "row", -1)
    b_full = place(b_full, b_o0, (row + 2) % n_row * own, 0)
    b_full = place(b_full, b_o1, (row + 2) % n_row * own + half, 0)
    mine = jnp.zeros((n_z, n_x, 4 * om_rows, kept), omega.dtype)
    for block, d in ((by_z, 0), (left, 1), (right, -1)):
        mine = place(mine, block[:, None], (x - d) % n_x, 1)
    mine = lax.dynamic_update_slice(mine, far_a[:, None], (0, (x + 2) % n_x, 0, 0))
    mine = lax.dynamic_update_slice(mine, far_b[:, None], (n_z // 2, (x + 2) % n_x, 0, 0))
    th0 = theta_of(gate, b_full, [a0], (0,), own)
    al, ar, th0 = tie((al, ar, th0))
    other = rot(mine, "bond_2", 1)
    om = jnp.stack([jnp.where(core == 0, mine, other), jnp.where(core == 0, other, mine)], axis=2)
    om = om.reshape(-1, kept)
    th1 = theta_of(gate, b_full, [al, ar], (0, 0), own)
    om, th1 = tie((om, th1))
    sketch, gram = sketch_gram(om, [th0, th1], 2 * n_row * own)
    gram, a_o0, a_o1 = tie((gram, a_o0, a_o1))
    th2, sketch, gram = last_chunk(gate, b_full, om, [a_o0, a_o1], sketch, gram)
    next_sketch = from_behind(sketch)
    yh, yl, packed = chol_inverse(gram, 2.0 * bond_width)
    next_packed = from_behind(packed)
    left_new, right_new, mid_h, mid_l = project(
        row, yh, yl, sketch, [th0, th1, th2], next_sketch, (0, 3, 1, 2)
    )
    odd_pair = odd_product(mid_h, mid_l, next_packed)
    return (left_new, right_new, odd_pair)


def solution(mesh):
    torus = Mesh(
        mesh.devices.reshape(8, 4, 2, mesh.shape["row"]), ("bond_0", "bond_1", "bond_2", "row")
    )
    in_specs = (P(BOND_ROW, None), P(BOND_ROW, None), P(), P(BOND_ROW, None))
    out_specs = (P(BOND_ROW, None), P(BOND_ROW, None), P(BOND_ROW, None))
    return jax.shard_map(
        shards, mesh=torus, in_specs=in_specs, out_specs=out_specs, check_vma=False
    )
```

```python
import functools
import math

import jax
import jax.numpy as jnp
from jax import lax
from jax.experimental import pallas as pl
from jax.experimental.pallas import tpu as pltpu
from jax.sharding import Mesh
from jax.sharding import PartitionSpec as P

BOND_ROW = ("bond_0", "bond_1", "bond_2", "row")
BOND = ("bond_0", "bond_1", "bond_2")
NB = 128


def sub_row(x, c):
    return jnp.broadcast_to(x[c:c+1, :], x.shape)
def lane_col(x, c):
    return jnp.broadcast_to(x[:, c:c+1], x.shape)
def diag_inverse(block):
    groups = NB // 8
    sub = lax.broadcasted_iota(jnp.int32, (8, NB), 0)
    lane = lax.broadcasted_iota(jnp.int32, (8, NB), 1)
    rows = [block[8*r:8*r+8, :] for r in range(groups)]
    er = [jnp.where(lane == sub + 8*r, 1.0, 0.0).astype(jnp.float32) for r in range(groups)]
    out = []
    for p in range(groups):
        cols = [lane_col(rows[p], 8*p+c) for c in range(8)]
        ahead = {r: [lane_col(rows[r], 8*p+c) for c in range(8)] for r in range(p+1, groups)}
        R, E = rows[p], er[p]
        raw = E; pv = cols[0]
        for c in range(0, 8, 2):
            k0, k1 = cols[c], cols[c+1]
            h0 = sub == c; h1 = sub == c+1; hh = h0 | h1
            p00 = sub_row(k0, c); p10 = sub_row(k0, c+1); p11 = sub_row(k1, c+1)
            det = p00*p11 - p10*p10
            r0 = 1.0 / (p00*det)
            rdet = r0*p00
            rp = r0*det
            i00 = p11*rdet; i01 = -p10*rdet; i11 = p00*rdet
            f = p10*rp
            m0 = jnp.where(hh, jnp.where(h0, -i00, -i01), k0*i00 + k1*i01)
            m1 = jnp.where(hh, jnp.where(h0, -i01, -i11), k0*i01 + k1*i11)
            pv = jnp.where(h0, p00, jnp.where(h1, det*rp, pv))
            e0, e1 = sub_row(E, c), sub_row(E, c+1)
            raw = jnp.where(h0, e0, jnp.where(h1, e1 - f*e0, raw))
            if p + 1 < groups:
                R = jnp.where(hh, 0.0, R) - m0*sub_row(R, c) - m1*sub_row(R, c+1)
            E = jnp.where(hh, 0.0, E) - m0*e0 - m1*e1
            for k in range(c+2, 8):
                q = cols[k]
                cols[k] = jnp.where(hh, 0.0, q) - m0*sub_row(q, c) - m1*sub_row(q, c+1)
        out.append(raw * lax.rsqrt(pv))
        if p + 1 < groups:
            rb = [sub_row(R, c) for c in range(8)]; eb = [sub_row(E, c) for c in range(8)]
            for r in range(p+1, groups):
                a, e = rows[r], er[r]
                for c in range(8):
                    a = a - ahead[r][c]*rb[c]
                    e = e - ahead[r][c]*eb[c]
                rows[r], er[r] = a, e
    return jnp.concatenate(out, axis=0)
def hi_lo(x):
    hi = x.astype(jnp.bfloat16)
    return hi, (x - hi.astype(jnp.float32)).astype(jnp.bfloat16)
NT = (((1,), (1,)), ((), ()))
NN = (((1,), (0,)), ((), ()))
def mm3(ah, al, bh, bl, dims):
    d = functools.partial(lax.dot_general, dimension_numbers=dims, preferred_element_type=jnp.float32)
    return d(ah, bh) + (d(ah, bl) + d(al, bh))
def chol_kernel(rows_summed, g_ref, yh_ref, yl_ref, packed_ref, lh, ll, d_ref, inv_ref, cpre, epre):
    n = g_ref.shape[0]
    nblk = n // NB
    i0 = lax.broadcasted_iota(jnp.int32, (NB, NB), 0)
    i1 = lax.broadcasted_iota(jnp.int32, (NB, NB), 1)
    eye = jnp.where(i0 == i1, 1.0, 0.0).astype(jnp.float32)
    tot = jnp.zeros((NB, NB), jnp.float32)
    for b in range(nblk):
        tot = tot + g_ref[b*NB:(b+1)*NB, b*NB:(b+1)*NB]*eye
    trace = jnp.sum(tot)
    tv = jnp.full((8, NB), trace)
    alpha = (n / tv)[0:1, :]
    scale = lax.rsqrt(tv * (1.0/(rows_summed*n)))[0:1, :]
    lh[...] = jnp.zeros_like(lh); ll[...] = jnp.zeros_like(ll)
    yh_ref[...] = jnp.zeros_like(yh_ref); yl_ref[...] = jnp.zeros_like(yl_ref)
    d_ref[...] = g_ref[0:NB, 0:NB]*alpha + 0.01*eye
    cpre[...] = jnp.zeros_like(cpre)
    epre[...] = jnp.zeros_like(epre)
    inv_ref[...] = jnp.zeros_like(inv_ref)
    rowid = lax.broadcasted_iota(jnp.int32, (n, NB), 0)
    def finish(b, depth):
        prev = pl.multiple_of(b*NB, NB)
        ih, il = hi_lo(inv_ref[...])
        epre[:, pl.ds(prev, NB)] = eye*scale
        eh, el = hi_lo(epre[:, :depth])
        yh, yl = hi_lo(mm3(ih, il, eh, el, NN))
        yh_ref[pl.ds(prev, NB), :depth] = yh
        yl_ref[pl.ds(prev, NB), :depth] = yl
        return ih, il, prev
    def body(low, depth, b, carry):
        block = d_ref[...]
        inv = diag_inverse(block)
        prevb = jnp.maximum(b-1, 0)
        ih, il, prev = finish(prevb, depth)
        ch, cl = hi_lo(cpre[low:, :])
        panel = jnp.where(rowid[low:] >= b*NB, mm3(ch, cl, ih, il, NT), 0.0)
        ph, plo = hi_lo(panel)
        lh[low:, pl.ds(prev, NB)] = ph
        ll[low:, pl.ds(prev, NB)] = plo
        cur = pl.multiple_of(b*NB, NB)
        rh, rl = lh[pl.ds(cur, NB), :depth], ll[pl.ds(cur, NB), :depth]
        cpre[low:, :] = g_ref[low:, pl.ds(cur, NB)]*alpha - mm3(lh[low:, :depth], ll[low:, :depth], rh, rl, NT)
        epre[:, :depth] = -mm3(rh, rl, yh_ref[:depth, :depth], yl_ref[:depth, :depth], NN)
        nxt = pl.multiple_of(jnp.minimum(b+1, nblk-1)*NB, NB)
        nh, nl = lh[pl.ds(nxt, NB), :depth], ll[pl.ds(nxt, NB), :depth]
        dpre = g_ref[pl.ds(nxt, NB), pl.ds(nxt, NB)]*alpha + 0.01*eye - mm3(nh, nl, nh, nl, NT)
        inv_ref[...] = inv
        vh, vl = hi_lo(inv)
        xh, xl = hi_lo(cpre[pl.ds(nxt, NB), :])
        th, tl = hi_lo(mm3(xh, xl, vh, vl, NT))
        d_ref[...] = dpre - mm3(th, tl, th, tl, NT)
        return carry
    per = nblk // 2
    for seg in range(2):
        lax.fori_loop(seg*per, (seg+1)*per, functools.partial(body, seg*per*NB, (seg+1)*per*NB), 0)
    finish(nblk-1, n)
    q = n // 4
    packed_ref[:q, :n] = yh_ref[3*q:, :]
    packed_ref[:q, n:] = yh_ref[:q, :q]
    packed_ref[q:, :3*q] = yh_ref[2*q:3*q, :3*q]
    packed_ref[q:, 3*q:] = yh_ref[q:2*q, :2*q]
def chol_inverse(gram_sum, rows_summed):
    n = gram_sum.shape[0]
    return pl.pallas_call(
        functools.partial(chol_kernel, rows_summed),
        out_shape=[jax.ShapeDtypeStruct((n, n), jnp.bfloat16)]*2 + [jax.ShapeDtypeStruct((n//2, 5*n//4), jnp.bfloat16)],
        in_specs=[pl.BlockSpec(memory_space=pltpu.VMEM)],
        out_specs=[pl.BlockSpec(memory_space=pltpu.VMEM)]*3,
        scratch_shapes=[pltpu.VMEM((n,n),jnp.bfloat16)]*2+[pltpu.VMEM((NB,NB),jnp.float32)]*2+[pltpu.VMEM((n,NB),jnp.float32),pltpu.VMEM((NB,n),jnp.float32)],
        name="chol_inverse",
        cost_estimate=pl.CostEstimate(flops=6*10**10, transcendentals=0, bytes_accessed=10*2**20),
        compiler_params=pltpu.CompilerParams(vmem_limit_bytes=18 * 1024 * 1024),
    )(gram_sum)


TN = (((0,), (0,)), ((), ()))
MIB = 1024 * 1024


def f32_dot(a, b, dims=NN):
    return lax.dot_general(a, b, dims, preferred_element_type=jnp.float32)


def in_vmem():
    return pl.BlockSpec(memory_space=pltpu.VMEM)


def in_place():
    return pl.BlockSpec(memory_space=pltpu.HBM)


def in_smem():
    return pl.BlockSpec(memory_space=pltpu.SMEM)


def limit(mib):
    return pltpu.CompilerParams(vmem_limit_bytes=mib * MIB)


def cost(gflop, mib):
    return pl.CostEstimate(flops=gflop * 10**9, transcendentals=0, bytes_accessed=mib * MIB)


def mix(gate_ref, spins, b_ref, th_ref, first):
    half = b_ref.shape[1] // 2
    width = 256
    for c in range(0, half, width):
        p = {}
        for v in range(2):
            cols = slice(v * half + c, v * half + c + width)
            for u in range(2):
                p[u, v] = f32_dot(spins(u), b_ref[:, cols])
        rows = p[0, 0].shape[0]
        for s in range(2):
            for t in range(2):
                mixed = None
                for u in range(2):
                    for v in range(2):
                        term = gate_ref[2 * s + t, 2 * u + v] * p[u, v]
                        mixed = term if mixed is None else mixed + term
                r = first + s * rows
                th_ref[r : r + rows, t * half + c : t * half + c + width] = mixed.astype(jnp.bfloat16)


def sketch_of(th_ref, om_ref, s_ref, first):
    rows = th_ref.shape[0]
    for k in range(0, om_ref.shape[1], 256):
        s_ref[first : first + rows, k : k + 256] = f32_dot(
            th_ref[...], om_ref[:, k : k + 256]
        ).astype(jnp.bfloat16)


def gram_of(s_ref, first, end, g_ref, add):
    for k in range(0, g_ref.shape[0], 256):
        total = f32_dot(s_ref[first:end, k:], s_ref[first:end, k : k + 256], TN)
        if add:
            total = g_ref[k:, k : k + 256] + total
        g_ref[k:, k : k + 256] = total


def theta_kernel(starts, rows, gate_ref, b_ref, *refs):
    depth = b_ref.shape[0]
    for j, (a_ref, r) in enumerate(zip(refs[:-1], starts)):
        mix(
            gate_ref,
            lambda u: a_ref[r : r + rows, u * depth : (u + 1) * depth],
            b_ref,
            refs[-1],
            2 * j * rows,
        )


def theta_of(gate, b_full, blocks, starts, rows):
    return pl.pallas_call(
        functools.partial(theta_kernel, starts, rows),
        out_shape=jax.ShapeDtypeStruct((2 * rows * len(blocks), b_full.shape[1]), jnp.bfloat16),
        in_specs=[in_smem()] + [in_vmem()] * (1 + len(blocks)),
        out_specs=in_vmem(),
        name="theta_of",
        cost_estimate=cost(9, 14),
        compiler_params=limit(18),
    )(gate, b_full, *blocks)


def gram_kernel(om_ref, *refs):
    th_refs, s_ref, g_ref = refs[:-2], refs[-2], refs[-1]
    end = 0
    for th_ref in th_refs:
        sketch_of(th_ref, om_ref, s_ref, end)
        end += th_ref.shape[0]
    gram_of(s_ref, 0, end, g_ref, False)


def sketch_gram(om, thetas, rows):
    kept = om.shape[1]
    return pl.pallas_call(
        gram_kernel,
        out_shape=[
            jax.ShapeDtypeStruct((rows, kept), jnp.bfloat16),
            jax.ShapeDtypeStruct((kept, kept), jnp.float32),
        ],
        in_specs=[in_vmem()] * (1 + len(thetas)),
        out_specs=[in_vmem()] * 2,
        name="sketch_gram",
        cost_estimate=cost(10, 17),
        compiler_params=limit(22),
    )(om, *thetas)


def last_kernel(gate_ref, b_ref, om_ref, a0_ref, a1_ref, sin_ref, gin_ref, *refs):
    th_hbm, s_ref, g_ref, th_ref, sem = refs
    depth = b_ref.shape[0]

    def spins(u):
        cols = slice(u * depth, (u + 1) * depth)
        return jnp.concatenate([a0_ref[:, cols], a1_ref[:, cols]], axis=0)

    mix(gate_ref, spins, b_ref, th_ref, 0)
    copy = pltpu.make_async_copy(th_ref, th_hbm, sem)
    copy.start()
    end = s_ref.shape[0]
    first = end - th_ref.shape[0]
    sketch_of(th_ref, om_ref, s_ref, first)
    gram_of(s_ref, first, end, g_ref, True)
    copy.wait()


def last_chunk(gate, b_full, om, halves, sketch, gram):
    rows = 4 * halves[0].shape[0]
    return pl.pallas_call(
        last_kernel,
        out_shape=[
            jax.ShapeDtypeStruct((rows, b_full.shape[1]), jnp.bfloat16),
            jax.ShapeDtypeStruct(sketch.shape, jnp.bfloat16),
            jax.ShapeDtypeStruct(gram.shape, jnp.float32),
        ],
        in_specs=[in_smem()] + [in_vmem()] * 6,
        out_specs=[in_place()] + [in_vmem()] * 2,
        scratch_shapes=[
            pltpu.VMEM((rows, b_full.shape[1]), jnp.bfloat16),
            pltpu.SemaphoreType.DMA,
        ],
        input_output_aliases={5: 1, 6: 2},
        name="last_chunk",
        cost_estimate=cost(7, 20),
        compiler_params=limit(32),
    )(gate, b_full, om, *halves, sketch, gram)


def project_kernel(offsets, right_scale, pair_scale, *refs):
    row_ref, yh_ref, yl_ref, s_ref = refs[:4]
    th_hbm, next_hbm = refs[4:7], refs[7]
    left_ref, right_ref, mid_h, mid_l, basis_ref, wide_ref, th_ref, next_ref, sems = refs[8:17]
    row = row_ref[0]
    kept = yh_ref.shape[0]
    rows = right_ref.shape[0]
    copies = []
    first = 0
    for i, src in enumerate(th_hbm):
        dst = th_ref.at[pl.ds(first, src.shape[0]), :]
        copies.append(pltpu.make_async_copy(src, dst, sems.at[i]))
        copies[-1].start()
        first += src.shape[0]
    next_copy = pltpu.make_async_copy(next_hbm, next_ref, sems.at[3])
    next_copy.start()
    mine = pl.ds(pl.multiple_of(row * rows, rows), rows)
    for first in range(0, s_ref.shape[0], 2 * rows):
        part = slice(first, first + 2 * rows)
        basis_ref[part, :] = (
            f32_dot(s_ref[part, :], yh_ref[mine, :], NT) + f32_dot(s_ref[part, :], yl_ref[mine, :], NT)
        ).astype(jnp.bfloat16)
    for c in range(0, kept, 256):
        own = slice(0, 2 * rows)
        left = f32_dot(s_ref[own, : c + 256], yh_ref[c : c + 256, : c + 256], NT) + f32_dot(
            s_ref[own, : c + 256], yl_ref[c : c + 256, : c + 256], NT
        )
        for i in range(2):
            block = c // NB + i
            for s in range(2):
                wide_ref[block, pl.ds(s, rows, stride=2), :] = left[
                    s * rows : (s + 1) * rows, i * NB : (i + 1) * NB
                ]
            left_ref[:, block * NB : (block + 1) * NB] = wide_ref[block].astype(jnp.bfloat16)
    for copy in copies:
        copy.wait()
    width = right_ref.shape[1]
    for c in range(0, width, 256):
        total = f32_dot(basis_ref[...], th_ref[:, c : c + 256], TN)
        right_ref[:, c : c + 256] = (total * right_scale).astype(jnp.bfloat16)
    next_copy.wait()
    for t in range(2):
        parts = []
        for d in offsets:
            start = t * (width // 2) + lax.rem(row + d, 4) * rows
            parts.append(pl.ds(pl.multiple_of(start, rows), rows))
        for s in range(2):
            for c in range(0, kept, 256):
                total = None
                for j in range(4):
                    r = (2 * j + s) * rows
                    term = f32_dot(right_ref[:, parts[j]], next_ref[r : r + rows, c : c + 256])
                    total = term if total is None else total + term
                total = total * pair_scale
                for i in range(2):
                    block = (s * kept + c) // NB + i
                    wide_ref[block, pl.ds(t, rows, stride=2), :] = total[:, i * NB : (i + 1) * NB]
    for c in range(2 * kept // NB):
        high, low = hi_lo(wide_ref[c])
        mid_h[:, c * NB : (c + 1) * NB] = high
        mid_l[:, c * NB : (c + 1) * NB] = low


def project(row, yh, yl, sketch, thetas, next_sketch, offsets):
    total_rows, kept = sketch.shape
    rows = total_rows // 4
    width = thetas[0].shape[1]
    return pl.pallas_call(
        functools.partial(
            project_kernel, offsets, 1.0 / math.sqrt(1.0 * width), 1.0 / math.sqrt(0.5 * width)
        ),
        out_shape=[
            jax.ShapeDtypeStruct((rows, kept), jnp.bfloat16),
            jax.ShapeDtypeStruct((rows // 2, width), jnp.bfloat16),
            jax.ShapeDtypeStruct((rows, 2 * kept), jnp.bfloat16),
            jax.ShapeDtypeStruct((rows, 2 * kept), jnp.bfloat16),
        ],
        in_specs=[in_smem()] + [in_vmem()] * 3 + [in_place()] * 4,
        out_specs=[in_vmem()] * 4,
        scratch_shapes=[
            pltpu.VMEM((total_rows, rows // 2), jnp.bfloat16),
            pltpu.VMEM((2 * kept // NB, rows, NB), jnp.float32),
            pltpu.VMEM((total_rows, width), jnp.bfloat16),
            pltpu.VMEM((total_rows, kept), jnp.bfloat16),
            pltpu.SemaphoreType.DMA((4,)),
        ],
        name="project",
        cost_estimate=cost(9, 22),
        compiler_params=limit(34),
    )(row.reshape(1).astype(jnp.int32), yh, yl, sketch, *thetas, next_sketch)


def pair_kernel(mid_h, mid_l, packed, odd_ref):
    kept = packed.shape[1] * 4 // 5
    q = kept // 4
    corner = {0: (0, kept), 1: (q, 3 * q), 2: (q, 0), 3: (0, 0)}
    for i in range(4):
        r0, c0 = corner[i]
        depth = (i + 1) * q
        for s in range(2):
            inv = packed[r0 : r0 + q, c0 : c0 + depth]
            out = f32_dot(mid_h[:, s * kept : s * kept + depth], inv, NT)
            out = out + f32_dot(mid_l[:, s * kept : s * kept + depth], inv, NT)
            odd_ref[:, s * kept + i * q : s * kept + (i + 1) * q] = out.astype(jnp.bfloat16)


def odd_product(mid_h, mid_l, packed):
    return pl.pallas_call(
        pair_kernel,
        out_shape=jax.ShapeDtypeStruct(mid_h.shape, jnp.bfloat16),
        in_specs=[in_vmem()] * 3,
        out_specs=in_vmem(),
        name="odd_product",
        cost_estimate=cost(3, 7),
        compiler_params=limit(16),
    )(mid_h, mid_l, packed)


def rot(block, axis, distance):
    count = lax.axis_size(axis)
    return lax.ppermute(block, axis, [(i, (i + distance) % count) for i in range(count)])


def from_behind(block):
    count = lax.axis_size(BOND)
    return lax.ppermute(block, BOND, [(i + 1, i) for i in range(count - 1)])


def place(whole, block, index, dim):
    starts = [0] * whole.ndim
    starts[dim] = index
    return lax.dynamic_update_slice(whole, block, tuple(starts))


def paired(block, axis, bit, dim):
    count = lax.axis_size(axis)
    other = lax.ppermute(block, axis, [(i, i ^ bit) for i in range(count)])
    low = (lax.axis_index(axis) & bit) == 0
    return jnp.stack([jnp.where(low, block, other), jnp.where(low, other, block)], axis=dim)


def shards(left_site, right_site, gate, omega):
    row_count, bond_width = left_site.shape
    own = right_site.shape[0]
    half = own // 2
    n_row = lax.axis_size("row")
    row = lax.axis_index("row")
    tie = lax.optimization_barrier
    om_rows, kept = omega.shape
    n_x, n_z = lax.axis_size("bond_1"), lax.axis_size("bond_0")
    x, core = lax.axis_index("bond_1"), lax.axis_index("bond_2")

    bl, br = rot(right_site, "row", 1), rot(right_site, "row", -1)
    strip = paired(paired(omega, "row", 1, 0), "row", 2, 0).reshape(4 * om_rows, kept)
    a0 = left_site.reshape(own, 2 * bond_width)
    strip = paired(paired(strip, "bond_0", 4, 0), "bond_0", 2, 1)
    strip, bl, br, a0 = tie((strip, bl, br, a0))
    b_o0, b_o1 = rot(bl[:half], "row", 1), rot(br[half:], "row", -1)
    al, ar = rot(a0, "row", 1), rot(a0, "row", -1)
    b_full = jnp.zeros((n_row * own, right_site.shape[1]), right_site.dtype)
    b_full = place(b_full, right_site, row * own, 0)
    b_full = place(b_full, bl, (row - 1) % n_row * own, 0)
    b_full = place(b_full, br, (row + 1) % n_row * own, 0)
    by_z = paired(strip, "bond_0", 1, 2).reshape(n_z, 4 * om_rows, kept)
    by_z, b_o0, b_o1 = tie((by_z, b_o0, b_o1))
    left, right = rot(by_z, "bond_1", 1), rot(by_z, "bond_1", -1)
    far_a = rot(left[: n_z // 2], "bond_1", 1)
    far_b = rot(right[n_z // 2 :], "bond_1", -1)
    a_o0, a_o1 = rot(al[:half], "row", 1), rot(ar[half:], "row", -1)
    b_full = place(b_full, b_o0, (row + 2) % n_row * own, 0)
    b_full = place(b_full, b_o1, (row + 2) % n_row * own + half, 0)
    mine = jnp.zeros((n_z, n_x, 4 * om_rows, kept), omega.dtype)
    for block, d in ((by_z, 0), (left, 1), (right, -1)):
        mine = place(mine, block[:, None], (x - d) % n_x, 1)
    mine = lax.dynamic_update_slice(mine, far_a[:, None], (0, (x + 2) % n_x, 0, 0))
    mine = lax.dynamic_update_slice(mine, far_b[:, None], (n_z // 2, (x + 2) % n_x, 0, 0))
    th0 = theta_of(gate, b_full, [a0], (0,), own)
    al, ar, th0 = tie((al, ar, th0))
    other = rot(mine, "bond_2", 1)
    om = jnp.stack([jnp.where(core == 0, mine, other), jnp.where(core == 0, other, mine)], axis=2)
    om = om.reshape(-1, kept)
    th1 = theta_of(gate, b_full, [al, ar], (0, 0), own)
    om, th1 = tie((om, th1))
    sketch, gram = sketch_gram(om, [th0, th1], 2 * n_row * own)
    gram, a_o0, a_o1 = tie((gram, a_o0, a_o1))
    th2, sketch, gram = last_chunk(gate, b_full, om, [a_o0, a_o1], sketch, gram)
    next_sketch = from_behind(sketch)
    yh, yl, packed = chol_inverse(gram, 2.0 * bond_width)
    next_packed = from_behind(packed)
    left_new, right_new, mid_h, mid_l = project(
        row, yh, yl, sketch, [th0, th1, th2], next_sketch, (0, 3, 1, 2)
    )
    odd_pair = odd_product(mid_h, mid_l, next_packed)
    return (left_new, right_new, odd_pair)


def solution(mesh):
    torus = Mesh(
        mesh.devices.reshape(8, 4, 2, mesh.shape["row"]), ("bond_0", "bond_1", "bond_2", "row")
    )
    in_specs = (P(BOND_ROW, None), P(BOND_ROW, None), P(), P(BOND_ROW, None))
    out_specs = (P(BOND_ROW, None), P(BOND_ROW, None), P(BOND_ROW, None))
    return jax.shard_map(
        shards, mesh=torus, in_specs=in_specs, out_specs=out_specs, check_vma=False
    )
```
